32 devices in a mesh: off: 16 (over z, y, x), dep: 2 (over core).
Axes of the slice: x: 2, y: 2, z: 4, core: 2. Of those that a mesh axis runs over, the one named last changes fastest.
Arguments:
- snapshots: bfloat16 [16, 8, 64, 256], P('off', 'dep'), may hold values from -6 to 6
- reflect: bfloat16 [192, 8, 64, 256], P('off', 'dep'), may hold values from -0.4375 to 0.4375
- courant: float32 [8, 64, 256], P('dep'), may hold values from 0.03 to 0.18
- lags: int32 [192], P('off'), may hold values from -32 to 32, as said below
- owners: int32 [8], replicated, may hold values from 0 to 15, as said below
Outputs:
- scattered: float32 [8, 64, 256], P('dep')
The draws below stay inside these ranges and needn't reach their ends.
Inputs may be any that keep to these rules, and one draw needn't show every extreme that they name: `lags`: some offset has lag -32 and some offset has lag 32. `owners`: some step uses wavefield 0 and some step uses wavefield 16 - 1.
All inputs are finite; a program needn't handle non-finite values.
Results may differ from the reference program's by a relative error of at most 0.0003.
Values may be sent and summed in bfloat16 or wider, within the bound.
No kernel may reach another device: no remote copies, remote signals or barrier semaphores. Data moves between devices by JAX's collectives and lax.ppermute only.
A program may use at most 64 MiB of HBM per device.

```python
import math
import jax
import jax.numpy as jnp
from jax import lax

NX = 256
NY = 64
ITERS = 8
LAG = 32
NOFF = 192
NZ = 8
NSNAP = 16


def draw_lags(key, part):
    first_key, second_key = jax.random.split(jax.random.fold_in(key, 17))
    values = jax.random.randint(first_key, (NOFF,), -LAG, LAG + 1)
    places = jax.random.permutation(second_key, NOFF)
    values = values.at[places[0]].set(-LAG).at[places[1]].set(LAG)
    return values.astype(jnp.int32)


def draw_owners(key, part):
    first_key, second_key = jax.random.split(jax.random.fold_in(key, 29))
    values = jax.random.randint(first_key, (ITERS,), 0, NSNAP)
    places = jax.random.permutation(second_key, ITERS)
    values = values.at[places[0]].set(0).at[places[1]].set(NSNAP - 1)
    return values.astype(jnp.int32)


def steps_of(rng, shape, pieces, smallest, high):
    def one(axis_at, shards_of):
        draws = jax.random.uniform(jax.random.fold_in(jax.random.fold_in(rng, 6), axis_at), (shards_of,), jnp.float32, smallest / len(pieces), high / len(pieces))
        return jnp.repeat(jnp.exp(draws), shape[axis_at] // shards_of).reshape((-1,) + (1,) * (len(shape) - axis_at - 1))

    factor_of = one(*pieces[0])
    for cut in pieces[1:]:
        factor_of = factor_of * one(*cut)
    return factor_of


def bell_draw(stream_key, extent, deviation, most, pieces=(), kind=jnp.bfloat16):
    level = steps_of(stream_key, extent, pieces, -0.22, 0.18) if pieces else 1.0
    drawn = jax.random.normal(stream_key, extent, jnp.float32) * deviation * level
    return jnp.minimum(jnp.maximum(drawn, -most), most).astype(kind)


def setup_inputs(seed: int = 0) -> dict:
    keys = jax.random.split(jax.random.key(seed), 6)
    return {
        "snapshots": bell_draw(keys[0], (NSNAP, NZ, NY, NX), 1.0, 6.0, ((0, 16), (1, 2))),
        "reflect": bell_draw(keys[1], (NOFF, NZ, NY, NX), NOFF ** -0.5, 0.4375, ((0, 16), (1, 2))),
        "courant": jnp.clip(jnp.exp(math.log(0.18) - 1.7917595 * jax.random.uniform(keys[2], (NZ, NY, NX), jnp.float32) ** steps_of(keys[2], (NZ, NY, NX), ((0, 2),), -0.2, 0.2)), 0.03, 0.18),
        "lags": draw_lags(jax.random.fold_in(keys[5], 71), 0),
        "owners": draw_owners(jax.random.fold_in(keys[5], 71), 0),
    }


STENCIL_WEIGHTS = (-205.0 / 72.0, 8.0 / 5.0, -1.0 / 5.0, 8.0 / 315.0, -1.0 / 560.0)


def stencil(padded, depth_cells, row_cells, column_cells):
    center = padded[4:4 + depth_cells, 4:4 + row_cells, 4:4 + column_cells]
    summed = (3.0 * STENCIL_WEIGHTS[0]) * center
    for distance in range(1, 5):
        neighbours = padded[4 + distance:4 + distance + depth_cells, 4:4 + row_cells, 4:4 + column_cells] + padded[4 - distance:4 - distance + depth_cells, 4:4 + row_cells, 4:4 + column_cells]
        neighbours = neighbours + padded[4:4 + depth_cells, 4 + distance:4 + distance + row_cells, 4:4 + column_cells] + padded[4:4 + depth_cells, 4 - distance:4 - distance + row_cells, 4:4 + column_cells]
        neighbours = neighbours + padded[4:4 + depth_cells, 4:4 + row_cells, 4 + distance:4 + distance + column_cells] + padded[4:4 + depth_cells, 4:4 + row_cells, 4 - distance:4 - distance + column_cells]
        summed = summed + STENCIL_WEIGHTS[distance] * neighbours
    return summed


def laplace(field):
    return stencil(jnp.pad(field, 4), field.shape[0], field.shape[1], field.shape[2])


def shifted_sum(reflect, acceleration, lags):
    width_cells = acceleration.shape[2]
    padded = jnp.pad(acceleration, ((0, 0), (0, 0), (LAG, LAG)))

    def add_offset(offset_index, summed):
        lag_now = lags[offset_index].astype(jnp.int32)
        window = lax.dynamic_slice_in_dim(padded, (LAG - lag_now).astype(jnp.int32), width_cells, 2)
        return summed + reflect[offset_index].astype(jnp.float32) * window

    return lax.fori_loop(0, reflect.shape[0], add_offset, jnp.zeros(acceleration.shape, acceleration.dtype))


def reference(snapshots, reflect, courant, lags, owners):
    scattered = jnp.zeros(courant.shape, courant.dtype)
    previous = jnp.zeros(courant.shape, courant.dtype)
    for step_now in range(ITERS):
        background = snapshots[owners[step_now]].astype(jnp.float32)
        acceleration = courant * laplace(background)
        source = shifted_sum(reflect, acceleration, lags)
        updated = 2.0 * scattered - previous + courant * laplace(scattered) + source
        previous = scattered
        scattered = updated
    return scattered
```

```python
import functools

import jax
import jax.numpy as jnp
from jax import lax
from jax.experimental import pallas as pl
from jax.experimental.pallas import tpu as pltpu
from jax.sharding import PartitionSpec as P

ITERS = 8
LAG = 32
REACH = 4

STENCIL_WEIGHTS = (-205.0 / 72.0, 8.0 / 5.0, -1.0 / 5.0, 8.0 / 315.0, -1.0 / 560.0)


BF16 = jnp.bfloat16
F32 = jnp.float32


def extended(cells, sides, width):
    for axis, dim in sides:
        count = lax.axis_size(axis)
        ends = count - 1
        head = lax.slice_in_dim(cells, 0, width, axis=dim)
        tail = lax.slice_in_dim(cells, cells.shape[dim] - width, cells.shape[dim], axis=dim)
        cells = jnp.concatenate(
            [
                lax.ppermute(tail, axis, [(i, (i + 1) % count) for i in range(ends)]),
                cells,
                lax.ppermute(head, axis, [((i + 1) % count, i) for i in range(ends)]),
            ],
            axis=dim,
        )
    return cells


def broadcast(x, axis, root):
    mine = lax.axis_index(axis) == root
    return lax.psum(jnp.where(mine, x, jnp.zeros_like(x)), axis)


def stencil(padded, depth_cells, row_cells, column_cells):
    def part(dz, dy, dx):
        return padded[
            4 + dz : 4 + dz + depth_cells, 4 + dy : 4 + dy + row_cells, 4 + dx : 4 + dx + column_cells
        ]

    summed = 3.0 * STENCIL_WEIGHTS[0] * part(0, 0, 0)
    for k in range(1, 5):
        neighbours = part(k, 0, 0) + part(-k, 0, 0)
        neighbours = neighbours + part(0, k, 0) + part(0, -k, 0)
        neighbours = neighbours + part(0, 0, k) + part(0, 0, -k)
        summed = summed + STENCIL_WEIGHTS[k] * neighbours
    return summed


def shifted_sum(reflect, acceleration, lags):
    width_cells = acceleration.shape[2]
    padded = jnp.pad(acceleration, ((0, 0), (0, 0), (LAG, LAG)))

    def add_offset(offset_index, summed):
        lag_now = lags[offset_index]
        window = lax.dynamic_slice_in_dim(padded, LAG - lag_now, width_cells, 2)
        return summed + reflect[offset_index].astype(F32) * window

    return lax.fori_loop(0, reflect.shape[0], add_offset, jnp.zeros(acceleration.shape, F32))


def halo_steps(snapshots, reflect, courant, lags, owners):
    own_layers = extended(snapshots[0], (("dep", 0),), 4)
    own_ready = courant * stencil(
        jnp.pad(own_layers, ((0, 0), (4, 4), (4, 4))).astype(F32), *courant.shape
    )
    scattered = jnp.zeros(courant.shape, F32)
    previous = jnp.zeros(courant.shape, F32)
    for step_now in range(ITERS):
        acceleration = broadcast(own_ready, "off", owners[step_now])
        source = shifted_sum(reflect, acceleration, lags)
        field = jnp.pad(extended(scattered, (("dep", 0),), 4), ((0, 0), (4, 4), (4, 4)))
        updated = 2.0 * scattered - previous + courant * stencil(field, *courant.shape) + source
        previous = scattered
        scattered = updated
    return lax.psum(scattered, "off")


def split(v):
    high = v.astype(BF16)
    return high, (v - high.astype(F32)).astype(BF16)


def band(rows, columns, block):
    i = lax.broadcasted_iota(jnp.int32, (rows, columns), 0)
    j = lax.broadcasted_iota(jnp.int32, (rows, columns), 1)
    apart = jnp.where(i // block == j // block, jnp.abs(i - j), 0)
    full = jnp.zeros((rows, columns), F32)
    for k in range(1, REACH + 1):
        full = jnp.where(apart == k, STENCIL_WEIGHTS[k], full)
    return split(full)


def born_kernel(
    where_ref,
    owners_ref,
    lags_ref,
    banks,
    own_reflect,
    far_reflect,
    own_courant,
    far_courant,
    kept_ref,
    given_ref,
    fields,
    refl,
    cour,
    across,
    down,
    lap,
    acc4,
    source,
    wave,
    sems,
):
    place, core = where_ref[0], where_ref[1]
    half = own_courant.shape[0]
    depth, rows, columns = cour.shape
    offsets = refl.shape[0]
    here, there = core * half, (1 - core) * half
    first = core * offsets

    local = [
        pltpu.make_async_copy(own_courant, cour.at[pl.ds(here, half)], sems.at[0]),
        pltpu.make_async_copy(far_courant, cour.at[pl.ds(there, half)], sems.at[1]),
        pltpu.make_async_copy(own_reflect.at[pl.ds(first, offsets)], refl.at[:, pl.ds(here, half)], sems.at[2]),
        pltpu.make_async_copy(far_reflect, refl.at[:, pl.ds(there, half)], sems.at[3]),
    ]
    for c in local:
        c.start()

    for t in range(ITERS):
        apart = owners_ref[t] ^ place
        low = apart % 4
        line = apart // 4
        for test, at, own, far in banks(low, line):

            @pl.when(test)
            def _(at=at, own=own, far=far):
                pltpu.make_async_copy(own.at[at], fields.at[t, pl.ds(here, half)], sems.at[4 + 2 * t]).start()
                pltpu.make_async_copy(far.at[at], fields.at[t, pl.ds(there, half)], sems.at[5 + 2 * t]).start()

    wide_high, wide_low = band(columns, columns, columns)
    across[0:columns] = wide_high
    across[columns : 2 * columns] = wide_low
    across[2 * columns : 3 * columns] = wide_high
    group = down.shape[0]
    tall_high, tall_low = band(group, group, rows)
    down[:, 0:group] = tall_high
    down[:, group : 2 * group] = tall_low
    down[:, 2 * group : 3 * group] = tall_high
    acc4[0] = jnp.zeros(acc4.shape[1:], F32)
    acc4[3] = jnp.zeros(acc4.shape[1:], F32)
    for c in local:
        c.wait()

    planes = group // rows

    def sideways(plane_of, parts):
        for g in range(depth // planes):
            pieces = [plane_of(g * planes + p) for p in range(planes)]
            high = jnp.concatenate([p[0] for p in pieces], 0)
            terms = [high, high]
            if parts == 2:
                terms.append(jnp.concatenate([p[1] for p in pieces], 0))
            n = len(terms)
            x_part = jnp.dot(jnp.concatenate(terms, 1), across[0 : n * columns], preferred_element_type=F32)
            y_part = jnp.dot(down[:, 0 : n * group], jnp.concatenate(terms, 0), preferred_element_type=F32)
            both = x_part + y_part
            for p in range(planes):
                lap[g * planes + p] = both[p * rows : (p + 1) * rows]

    def vertical(plane_of, z):
        total = (3.0 * STENCIL_WEIGHTS[0]) * plane_of(z)
        for k in range(1, REACH + 1):
            near = [plane_of(n) for n in (z - k, z + k) if 0 <= n < depth]
            if near:
                total = total + STENCIL_WEIGHTS[k] * functools.reduce(jnp.add, near)
        return total

    lane = lax.broadcasted_iota(jnp.int32, (rows, 128), 1)

    def step(t, carry):
        now, before = t % 2, (t + 1) % 2
        pltpu.make_async_copy(fields.at[t, pl.ds(0, half)], fields.at[t, pl.ds(0, half)], sems.at[4 + 2 * t]).wait()
        pltpu.make_async_copy(fields.at[t, pl.ds(0, half)], fields.at[t, pl.ds(0, half)], sems.at[5 + 2 * t]).wait()
        sideways(lambda z: (fields[t, z], None), 1)
        for z in range(depth):
            plane = cour[z] * (lap[z] + vertical(lambda n: fields[t, n].astype(F32), z))
            acc4[1, z] = plane[:, 0:128]
            acc4[2, z] = plane[:, 128:256]
        for z in range(depth):
            left = jnp.zeros((rows, 128), F32)
            right = jnp.zeros((rows, 128), F32)
            for h in range(offsets):
                lag = lags_ref[first + h]
                negative = (lag < 0).astype(jnp.int32)
                turn = lag + 128 * negative
                keep = lane >= turn
                parts = [pltpu.roll(acc4[negative + i, z], turn, 1) for i in range(3)]
                image = refl[h, z].astype(F32)
                left = left + image[:, 0:128] * jnp.where(keep, parts[1], parts[0])
                right = right + image[:, 128:256] * jnp.where(keep, parts[2], parts[1])
            source[z, :, 0:128] = left
            source[z, :, 128:256] = right

        @pl.when(t == 0)
        def _():
            wave[1] = source[...]
            wave[0] = jnp.zeros(source.shape, F32)

        @pl.when(t > 0)
        def _():
            sideways(lambda z: split(wave[now, z]), 2)
            for z in range(depth):
                grown = cour[z] * (lap[z] + vertical(lambda n: wave[now, n], z))
                wave[before, z] = (2.0 * wave[now, z] - wave[before, z]) + (grown + source[z])

        return carry

    lax.fori_loop(0, ITERS, step, 0)
    last = ITERS % 2
    kept_ref[...] = wave[last, pl.ds(here, half)]
    given_ref[...] = wave[last, pl.ds(there, half)]


def swap_cores(x):
    return lax.ppermute(x, "dep", [(0, 1), (1, 0)])


def flip(x, bits):
    count = lax.axis_size("off")
    return lax.ppermute(x, "off", [(i, i ^ bits) for i in range(count)])


def core_pair(snapshots, reflect, courant, lags, owners):
    count = lax.axis_size("off")
    lines = count // 4
    core = lax.axis_index("dep")
    mine = reflect.shape[0] // 2
    half, rows, columns = courant.shape

    own = snapshots
    zs = [own] + [flip(own, 4 * j) for j in range(1, lines)]
    sent = lax.dynamic_slice_in_dim(reflect, (1 - core) * mine, mine, 0)
    far_reflect = swap_cores(sent)
    far_courant = swap_cores(courant)
    cut = lines // 2
    a = jnp.concatenate(zs[:cut], 0)
    b = jnp.concatenate(zs[cut:], 0)
    a_x = flip(a, 1)
    b_y = flip(b, 2)
    a_pair = jnp.concatenate([a, a_x], 0)
    b_pair = jnp.concatenate([b, b_y], 0)
    a_y = flip(a_pair, 2)
    b_x = flip(b_pair, 1)
    owns = [a_pair, b_pair, a_y, b_x]
    fars = [swap_cores(v) for v in owns]

    def kernel(where_ref, owners_ref, lags_ref, *refs):
        own_banks, far_banks, rest = refs[:4], refs[4:8], refs[8:]

        def banks(low, line):
            in_a = line < cut
            at_a, at_b = line, line - cut
            y, x = low // 2, low % 2
            return [
                (in_a & (y == 0), at_a + cut * x, own_banks[0], far_banks[0]),
                (jnp.logical_not(in_a) & (x == 0), at_b + (lines - cut) * y, own_banks[1], far_banks[1]),
                (in_a & (y == 1), at_a + cut * x, own_banks[2], far_banks[2]),
                (jnp.logical_not(in_a) & (x == 1), at_b + (lines - cut) * y, own_banks[3], far_banks[3]),
            ]

        born_kernel(where_ref, owners_ref, lags_ref, banks, *rest)

    depth = 2 * half
    group = 256 if (depth * rows) % 256 == 0 and 256 % rows == 0 else rows
    smem = pl.BlockSpec(memory_space=pltpu.SMEM)
    anyspace = pl.BlockSpec(memory_space=pl.ANY)
    vmem = pl.BlockSpec(memory_space=pltpu.VMEM)
    place = jnp.stack([lax.axis_index("off"), core]).astype(jnp.int32)
    kept, given = pl.pallas_call(
        kernel,
        out_shape=[jax.ShapeDtypeStruct((half, rows, columns), F32)] * 2,
        in_specs=[smem] * 3 + [anyspace] * 12,
        out_specs=[vmem] * 2,
        scratch_shapes=[
            pltpu.VMEM((ITERS, depth, rows, columns), BF16),
            pltpu.VMEM((mine, depth, rows, columns), BF16),
            pltpu.VMEM((depth, rows, columns), F32),
            pltpu.VMEM((3 * columns, columns), BF16),
            pltpu.VMEM((group, 3 * group), BF16),
            pltpu.VMEM((depth, rows, columns), F32),
            pltpu.VMEM((4, depth, rows, 128), F32),
            pltpu.VMEM((depth, rows, columns), F32),
            pltpu.VMEM((2, depth, rows, columns), F32),
            pltpu.SemaphoreType.DMA((4 + 2 * ITERS,)),
        ],
        compiler_params=pltpu.CompilerParams(vmem_limit_bytes=40 << 20),
        cost_estimate=pl.CostEstimate(flops=10**9, bytes_accessed=8 << 20, transcendentals=0),
    )(place, owners, lags, *owns, *fars, reflect, far_reflect, courant, far_courant)

    total = kept + swap_cores(given)
    pieces = total.reshape(count, half * rows // count, columns)
    summed = lax.all_to_all(pieces, "off", 0, 0).sum(0)
    spread = jnp.broadcast_to(summed[None], pieces.shape)
    return lax.all_to_all(spread, "off", 0, 0).reshape(half, rows, columns)


def solution(mesh):
    offs, deps = mesh.shape["off"], mesh.shape["dep"]

    def per_device(snapshots, reflect, courant, lags, owners):
        fits = (
            deps == 2
            and offs == snapshots.shape[0] * offs
            and offs in (8, 16)
            and reflect.shape[0] % 2 == 0
            and courant.shape[2] == 256
            and (courant.shape[0] * courant.shape[1]) % (8 * offs) == 0
            and 256 % courant.shape[1] == 0
        )
        body = core_pair if fits else halo_steps
        return body(snapshots, reflect, courant, lags, owners)

    in_specs = (
        P("off", "dep", None, None),
        P("off", "dep", None, None),
        P("dep", None, None),
        P("off"),
        P(),
    )
    return jax.shard_map(
        per_device, mesh=mesh, in_specs=in_specs, out_specs=P("dep", None, None), check_vma=False
    )
```

```python
import functools

import jax
import jax.numpy as jnp
from jax import lax
from jax.experimental import pallas as pl
from jax.experimental.pallas import tpu as pltpu
from jax.sharding import PartitionSpec as P


ITERS = 8
LAG = 32
REACH = 4

STENCIL_WEIGHTS = (-205.0 / 72.0, 8.0 / 5.0, -1.0 / 5.0, 8.0 / 315.0, -1.0 / 560.0)


BF16 = jnp.bfloat16
F32 = jnp.float32


def extended(cells, sides, width):
    for axis, dim in sides:
        count = lax.axis_size(axis)
        ends = count - 1
        head = lax.slice_in_dim(cells, 0, width, axis=dim)
        tail = lax.slice_in_dim(cells, cells.shape[dim] - width, cells.shape[dim], axis=dim)
        cells = jnp.concatenate(
            [
                lax.ppermute(tail, axis, [(i, (i + 1) % count) for i in range(ends)]),
                cells,
                lax.ppermute(head, axis, [((i + 1) % count, i) for i in range(ends)]),
            ],
            axis=dim,
        )
    return cells


def broadcast(x, axis, root):
    mine = lax.axis_index(axis) == root
    return lax.psum(jnp.where(mine, x, jnp.zeros_like(x)), axis)


def stencil(padded, depth_cells, row_cells, column_cells):
    def part(dz, dy, dx):
        return padded[
            4 + dz : 4 + dz + depth_cells, 4 + dy : 4 + dy + row_cells, 4 + dx : 4 + dx + column_cells
        ]

    summed = 3.0 * STENCIL_WEIGHTS[0] * part(0, 0, 0)
    for k in range(1, 5):
        neighbours = part(k, 0, 0) + part(-k, 0, 0)
        neighbours = neighbours + part(0, k, 0) + part(0, -k, 0)
        neighbours = neighbours + part(0, 0, k) + part(0, 0, -k)
        summed = summed + STENCIL_WEIGHTS[k] * neighbours
    return summed


def shifted_sum(reflect, acceleration, lags):
    width_cells = acceleration.shape[2]
    padded = jnp.pad(acceleration, ((0, 0), (0, 0), (LAG, LAG)))

    def add_offset(offset_index, summed):
        lag_now = lags[offset_index]
        window = lax.dynamic_slice_in_dim(padded, LAG - lag_now, width_cells, 2)
        return summed + reflect[offset_index].astype(F32) * window

    return lax.fori_loop(0, reflect.shape[0], add_offset, jnp.zeros(acceleration.shape, F32))


def halo_steps(snapshots, reflect, courant, lags, owners):
    own_layers = extended(snapshots[0], (("dep", 0),), 4)
    own_ready = courant * stencil(
        jnp.pad(own_layers, ((0, 0), (4, 4), (4, 4))).astype(F32), *courant.shape
    )
    scattered = jnp.zeros(courant.shape, F32)
    previous = jnp.zeros(courant.shape, F32)
    for step_now in range(ITERS):
        acceleration = broadcast(own_ready, "off", owners[step_now])
        source = shifted_sum(reflect, acceleration, lags)
        field = jnp.pad(extended(scattered, (("dep", 0),), 4), ((0, 0), (4, 4), (4, 4)))
        updated = 2.0 * scattered - previous + courant * stencil(field, *courant.shape) + source
        previous = scattered
        scattered = updated
    return lax.psum(scattered, "off")


def split(v):
    high = v.astype(BF16)
    return high, (v - high.astype(F32)).astype(BF16)


def band(rows, columns, block):
    i = lax.broadcasted_iota(jnp.int32, (rows, columns), 0)
    j = lax.broadcasted_iota(jnp.int32, (rows, columns), 1)
    apart = jnp.where(i // block == j // block, jnp.abs(i - j), 0)
    full = jnp.zeros((rows, columns), F32)
    for k in range(1, REACH + 1):
        full = jnp.where(apart == k, STENCIL_WEIGHTS[k], full)
    return split(full)


def copy(source, target, sem):
    return pltpu.make_async_copy(source, target, sem)


def prepare_kernel(core_ref, own_reflect, far_reflect, own_courant, far_courant, rt, cour, across, down, refl, sems):
    core = core_ref[0]
    half = own_courant.shape[0]
    rows, columns = cour.shape[1:]
    offsets, blocks = rt.shape[:2]
    stack = 128 // rows
    here, there = pl.ds(core * half, half), pl.ds((1 - core) * half, half)
    moves = [
        copy(own_courant, cour.at[here], sems.at[0]),
        copy(far_courant, cour.at[there], sems.at[1]),
        copy(own_reflect.at[pl.ds(core * offsets, offsets)], refl.at[:, here], sems.at[2]),
        copy(far_reflect, refl.at[:, there], sems.at[3]),
    ]
    for move in moves:
        move.start()
    high, low = band(columns, columns, columns)
    for i, part in enumerate((high, low, high)):
        across[i * columns : (i + 1) * columns] = part
    group = down.shape[0]
    high, low = band(group, group, rows)
    for i, part in enumerate((high, low, high)):
        down[:, i * group : (i + 1) * group] = part
    for move in moves:
        move.wait()

    def turn(h, carry):
        for b in range(blocks):
            tile = jnp.concatenate([refl[h, stack * b + i] for i in range(stack)], 0)
            rt[h, b] = tile.astype(F32).T.astype(BF16)
        return carry

    lax.fori_loop(0, offsets, turn, 0)


def vertical(plane_of, z, depth):
    total = (3.0 * STENCIL_WEIGHTS[0]) * plane_of(z)
    for k in range(1, REACH + 1):
        near = [plane_of(n) for n in (z - k, z + k) if 0 <= n < depth]
        if near:
            total = total + STENCIL_WEIGHTS[k] * functools.reduce(jnp.add, near)
    return total


def sideways(terms, across, down):
    n = len(terms)
    group, columns = terms[0].shape
    x_part = jnp.dot(jnp.concatenate(terms, 1), across[0 : n * columns], preferred_element_type=F32)
    y_part = jnp.dot(down[:, 0 : n * group], jnp.concatenate(terms, 0), preferred_element_type=F32)
    return x_part + y_part


def source_of(field, lag_of, rt, cour, across, down, plain, shifted, turned, source):
    depth, rows, columns = cour.shape
    offsets, blocks = rt.shape[:2]
    group = down.shape[0]
    planes, tiles, stack = group // rows, group // 128, 128 // rows
    for z in range(depth):
        plain[z] = field[z].astype(F32)
    for g in range(depth // planes):
        high = jnp.concatenate([field[g * planes + p] for p in range(planes)], 0)
        both = sideways([high, high], across, down)
        for b in range(tiles):
            pieces = []
            for i in range(stack):
                p = b * stack + i
                z = g * planes + p
                upright = vertical(lambda n: plain[n], z, depth)
                pieces.append(cour[z] * (both[p * rows : (p + 1) * rows] + upright))
            shifted[g * tiles + b, LAG : LAG + columns] = jnp.concatenate(pieces, 0).T
    chunk = 64
    for b in range(blocks):
        for r in range(0, columns, chunk):
            total = jnp.zeros((chunk, 128), F32)
            for h in range(offsets):
                image = rt[h, b, r : r + chunk].astype(F32)
                total = total + image * shifted[b, pl.ds(LAG + r - lag_of(h), chunk)]
            turned[b, r : r + chunk] = total
    for b in range(blocks):
        tile = turned[b].T
        for i in range(stack):
            source[stack * b + i] = tile[i * rows : (i + 1) * rows]


def clear_rims(shifted, columns):
    for b in range(shifted.shape[0]):
        shifted[b, 0:LAG] = jnp.zeros((LAG, 128), F32)
        shifted[b, LAG + columns : 2 * LAG + columns] = jnp.zeros((LAG, 128), F32)


def fetch_fields(where_ref, owners_ref, choose, fields, sems, half):
    place, core = where_ref[0], where_ref[1]
    here, there = pl.ds(core * half, half), pl.ds((1 - core) * half, half)
    for t in range(ITERS):
        for test, at, own, far in choose(owners_ref[t] ^ place):

            @pl.when(test)
            def _(at=at, own=own, far=far, t=t):
                copy(own.at[at], fields.at[t, here], sems.at[t, 0]).start()
                copy(far.at[at], fields.at[t, there], sems.at[t, 1]).start()


def held(where_ref, owners_ref, choose, t):
    tests = [test for test, *_ in choose(owners_ref[t] ^ where_ref[0])]
    return functools.reduce(jnp.logical_or, tests)


def wait_fields(fields, sems, t, half):
    for i in range(2):
        part = fields.at[t, pl.ds(i * half, half)]
        copy(part, part, sems.at[t, i]).wait()


def sums_kernel(
    choose, where_ref, owners_ref, lags_ref, rt, cour, across, down, sums,
    fields, plain, shifted, turned, field_sems,
):
    depth = cour.shape[0]
    first = where_ref[1] * rt.shape[0]
    fetch_fields(where_ref, owners_ref, choose, fields, field_sems, depth // 2)
    clear_rims(shifted, cour.shape[2])

    def step(t, carry):
        @pl.when(held(where_ref, owners_ref, choose, t))
        def _():
            wait_fields(fields, field_sems, t, depth // 2)
            source_of(
                fields.at[t], lambda h: lags_ref[first + h], rt, cour, across, down, plain, shifted, turned, sums.at[t]
            )

        return carry

    lax.fori_loop(0, ITERS, step, 0)


def steps_kernel(
    choose, where_ref, owners_ref, lags_ref, rt, cour, across, down, kept_ref, given_ref, sums,
    fields, plain, shifted, turned, field_sems, wave_a, wave_b,
):
    sums_kernel(
        choose, where_ref, owners_ref, lags_ref, rt, cour, across, down, sums,
        fields, plain, shifted, turned, field_sems,
    )
    depth, rows, _ = cour.shape
    half = depth // 2
    group = down.shape[0]
    planes = group // rows

    def grow(t, now, before):
        for g in range(depth // planes):
            high, low = split(jnp.concatenate([now[g * planes + p] for p in range(planes)], 0))
            both = sideways([high, high, low], across, down)
            for p in range(planes):
                z = g * planes + p
                laplace = both[p * rows : (p + 1) * rows] + vertical(lambda n: now[n], z, depth)
                before[z] = (2.0 * now[z] - before[z]) + (cour[z] * laplace + sums[t, z])

    wave_a[...] = sums[0]
    wave_b[...] = jnp.zeros(wave_b.shape, F32)

    def pair(i, carry):
        grow(2 * i + 1, wave_a, wave_b)
        grow(2 * i + 2, wave_b, wave_a)
        return carry

    lax.fori_loop(0, (ITERS - 1) // 2, pair, 0)
    last = wave_a
    if ITERS % 2 == 0:
        grow(ITERS - 1, wave_a, wave_b)
        last = wave_b
    core = where_ref[1]
    kept_ref[...] = last[pl.ds(core * half, half)]
    given_ref[...] = last[pl.ds((1 - core) * half, half)]


def swapped(x):
    return lax.ppermute(x, "dep", [(0, 1), (1, 0)])


def flip(x, bits):
    count = lax.axis_size("off")
    return lax.ppermute(x, "off", [(i, i ^ bits) for i in range(count)])


def core_pair(snapshots, reflect, courant, lags, owners):
    count = lax.axis_size("off")
    core = lax.axis_index("dep")
    mine = reflect.shape[0] // 2
    half, rows, columns = courant.shape
    depth = 2 * half
    blocks = depth * rows // 128
    group = 256
    wing = 4
    lines = count // wing
    cut = 2 * (lines - 1) // 3

    z_parts = [flip(snapshots, wing * j) for j in range(1, lines)]
    o_x, o_y = flip(snapshots, 1), flip(snapshots, 2)
    o_d = flip(o_x, 2)
    sent = lax.dynamic_slice_in_dim(reflect, (1 - core) * mine, mine, 0)
    far_reflect = swapped(sent)
    far_courant = swapped(courant)
    z_all = jnp.concatenate(z_parts, 0)
    z_x, z_y = flip(z_all, 1), flip(z_all, 2)
    d_x = flip(z_x[:cut], 2)
    d_y = flip(z_y[cut:], 1)

    smem = pl.BlockSpec(memory_space=pltpu.SMEM)
    anyspace = pl.BlockSpec(memory_space=pl.ANY)
    vmem = pl.BlockSpec(memory_space=pltpu.VMEM)
    where = jnp.stack([lax.axis_index("off"), core]).astype(jnp.int32)
    tables = [
        jax.ShapeDtypeStruct((mine, blocks, columns, 128), BF16),
        jax.ShapeDtypeStruct((depth, rows, columns), F32),
        jax.ShapeDtypeStruct((3 * columns, columns), BF16),
        jax.ShapeDtypeStruct((group, 3 * group), BF16),
    ]
    prepare = pl.pallas_call(
        prepare_kernel,
        out_shape=tables,
        in_specs=[smem] + [anyspace] * 4,
        out_specs=[vmem] * 4,
        scratch_shapes=[pltpu.VMEM((mine, depth, rows, columns), BF16), pltpu.SemaphoreType.DMA((4,))],
        compiler_params=pltpu.CompilerParams(vmem_limit_bytes=16 << 20),
        cost_estimate=pl.CostEstimate(flops=10**7, bytes_accessed=6 << 20, transcendentals=0),
    )
    prepared = prepare(where[1:], reflect, far_reflect, courant, far_courant)

    scratch = [
        pltpu.VMEM((ITERS, depth, rows, columns), BF16),
        pltpu.VMEM((depth, rows, columns), F32),
        pltpu.VMEM((blocks, columns + 2 * LAG, 128), F32),
        pltpu.VMEM((blocks, columns, 128), F32),
        pltpu.SemaphoreType.DMA((ITERS, 2)),
    ]
    waves = [pltpu.VMEM((depth, rows, columns), F32)] * 2
    params = pltpu.CompilerParams(vmem_limit_bytes=32 << 20)
    cost = pl.CostEstimate(flops=10**9, bytes_accessed=10 << 20, transcendentals=0)
    sums_shape = jax.ShapeDtypeStruct((ITERS, depth, rows, columns), F32)

    def near_banks(owns, fars):
        def choose(apart):
            low, line = apart % wing, apart // wing
            own_line = [((line == 0) & (low == i), 0, owns[i], fars[i]) for i in range(wing)]
            return own_line + [((line > 0) & (low == 0), line - 1, owns[wing], fars[wing])]

        return choose

    def side_banks(owns, fars):
        def choose(apart):
            low, line = apart % wing, apart // wing
            return [((line > 0) & (low == 1 + i), line - 1, owns[i], fars[i]) for i in range(2)]

        return choose

    def far_banks(owns, fars):
        def choose(apart):
            low, line = apart % wing, apart // wing
            return [
                ((low == 3) & (line > 0) & (line <= cut), line - 1, owns[0], fars[0]),
                ((low == 3) & (line > cut), line - 1 - cut, owns[1], fars[1]),
            ]

        return choose

    def run(body, banks, own_parts, extra, out_shape, more_scratch=()):
        far_parts = [swapped(v) for v in own_parts]
        n = len(own_parts)

        def kernel(where_ref, owners_ref, lags_ref, *refs):
            rest = refs[2 * n : 2 * n + 4] + refs[2 * n + 4 + len(extra) :]
            body(banks(refs[:n], refs[n : 2 * n]), where_ref, owners_ref, lags_ref, *rest)

        return pl.pallas_call(
            kernel,
            in_specs=[smem] * 3 + [anyspace] * (2 * n) + [vmem] * (4 + len(extra)),
            out_shape=out_shape,
            out_specs=[vmem] * len(out_shape),
            scratch_shapes=scratch + list(more_scratch),
            input_output_aliases={3 + 2 * n + 4: len(out_shape) - 1} if extra else {},
            compiler_params=params,
            cost_estimate=cost,
        )(where, owners, lags, *own_parts, *far_parts, *prepared, *extra)

    out_half = jax.ShapeDtypeStruct((half, rows, columns), F32)
    sums = run(sums_kernel, near_banks, [snapshots, o_x, o_y, o_d, z_all], [], [sums_shape])
    sums = run(sums_kernel, side_banks, [z_x, z_y], sums, [sums_shape])
    kept, given, _ = run(steps_kernel, far_banks, [d_x, d_y], sums, [out_half, out_half, sums_shape], waves)

    total = kept + swapped(given)
    pieces = total.reshape(count, half * rows // count, columns)
    summed = lax.all_to_all(pieces, "off", 0, 0).sum(0)
    spread = jnp.broadcast_to(summed[None], pieces.shape)
    return lax.all_to_all(spread, "off", 0, 0).reshape(half, rows, columns)


def solution(mesh):
    offs, deps = mesh.shape["off"], mesh.shape["dep"]

    def per_device(snapshots, reflect, courant, lags, owners):
        fits = (
            deps == 2
            and snapshots.shape[0] == 1
            and offs >= 16
            and offs & (offs - 1) == 0
            and reflect.shape[0] % 2 == 0
            and courant.shape[2] % 128 == 0
            and (courant.shape[0] * courant.shape[1]) % (8 * offs) == 0
            and (courant.shape[0] * courant.shape[1]) % 128 == 0
            and courant.shape[1] % 16 == 0
            and 128 % courant.shape[1] == 0
        )
        body = core_pair if fits else halo_steps
        return body(snapshots, reflect, courant, lags, owners)

    in_specs = (
        P("off", "dep", None, None),
        P("off", "dep", None, None),
        P("dep", None, None),
        P("off"),
        P(),
    )
    return jax.shard_map(
        per_device, mesh=mesh, in_specs=in_specs, out_specs=P("dep", None, None), check_vma=False
    )
```

```python
import functools

import jax
import jax.numpy as jnp
from jax import lax
from jax.experimental import pallas as pl
from jax.experimental.pallas import tpu as pltpu
from jax.sharding import PartitionSpec as P


ITERS = 8
LAG = 32
REACH = 4

STENCIL_WEIGHTS = (-205.0 / 72.0, 8.0 / 5.0, -1.0 / 5.0, 8.0 / 315.0, -1.0 / 560.0)


BF16 = jnp.bfloat16
F32 = jnp.float32


def extended(cells, sides, width):
    for axis, dim in sides:
        count = lax.axis_size(axis)
        ends = count - 1
        head = lax.slice_in_dim(cells, 0, width, axis=dim)
        tail = lax.slice_in_dim(cells, cells.shape[dim] - width, cells.shape[dim], axis=dim)
        cells = jnp.concatenate(
            [
                lax.ppermute(tail, axis, [(i, (i + 1) % count) for i in range(ends)]),
                cells,
                lax.ppermute(head, axis, [((i + 1) % count, i) for i in range(ends)]),
            ],
            axis=dim,
        )
    return cells


def broadcast(x, axis, root):
    mine = lax.axis_index(axis) == root
    return lax.psum(jnp.where(mine, x, jnp.zeros_like(x)), axis)


def stencil(padded, depth_cells, row_cells, column_cells):
    def part(dz, dy, dx):
        return padded[
            4 + dz : 4 + dz + depth_cells, 4 + dy : 4 + dy + row_cells, 4 + dx : 4 + dx + column_cells
        ]

    summed = 3.0 * STENCIL_WEIGHTS[0] * part(0, 0, 0)
    for k in range(1, 5):
        neighbours = part(k, 0, 0) + part(-k, 0, 0)
        neighbours = neighbours + part(0, k, 0) + part(0, -k, 0)
        neighbours = neighbours + part(0, 0, k) + part(0, 0, -k)
        summed = summed + STENCIL_WEIGHTS[k] * neighbours
    return summed


def shifted_sum(reflect, acceleration, lags):
    width_cells = acceleration.shape[2]
    padded = jnp.pad(acceleration, ((0, 0), (0, 0), (LAG, LAG)))

    def add_offset(offset_index, summed):
        lag_now = lags[offset_index]
        window = lax.dynamic_slice_in_dim(padded, LAG - lag_now, width_cells, 2)
        return summed + reflect[offset_index].astype(F32) * window

    return lax.fori_loop(0, reflect.shape[0], add_offset, jnp.zeros(acceleration.shape, F32))


def halo_steps(snapshots, reflect, courant, lags, owners):
    own_layers = extended(snapshots[0], (("dep", 0),), 4)
    own_ready = courant * stencil(
        jnp.pad(own_layers, ((0, 0), (4, 4), (4, 4))).astype(F32), *courant.shape
    )
    scattered = jnp.zeros(courant.shape, F32)
    previous = jnp.zeros(courant.shape, F32)
    for step_now in range(ITERS):
        acceleration = broadcast(own_ready, "off", owners[step_now])
        source = shifted_sum(reflect, acceleration, lags)
        field = jnp.pad(extended(scattered, (("dep", 0),), 4), ((0, 0), (4, 4), (4, 4)))
        updated = 2.0 * scattered - previous + courant * stencil(field, *courant.shape) + source
        previous = scattered
        scattered = updated
    return lax.psum(scattered, "off")


def split(v):
    high = v.astype(BF16)
    return high, (v - high.astype(F32)).astype(BF16)


EXACT_WEIGHTS = tuple(w / 4096.0 for w in (-43050.0, 8064.0, -1008.0, 128.0, -9.0))
SCALE = 4096.0 / 5040.0


def band(rows, columns, block):
    i = lax.broadcasted_iota(jnp.int32, (rows, columns), 0)
    j = lax.broadcasted_iota(jnp.int32, (rows, columns), 1)
    apart = jnp.where(i // block == j // block, jnp.abs(i - j), 0)
    full = jnp.zeros((rows, columns), F32)
    for k in range(1, REACH + 1):
        full = jnp.where(apart == k, EXACT_WEIGHTS[k], full)
    return full.astype(BF16)


def copy(source, target, sem):
    return pltpu.make_async_copy(source, target, sem)


def prepare_kernel(core_ref, own_reflect, far_reflect, own_courant, far_courant, rt, cour, across, down, refl, sems):
    core = core_ref[0]
    half = own_courant.shape[0]
    rows, columns = cour.shape[1:]
    offsets, blocks = rt.shape[:2]
    stack = 128 // rows
    here, there = pl.ds(core * half, half), pl.ds((1 - core) * half, half)
    mine = pl.ds(core * offsets, offsets)
    moves = [
        copy(own_reflect.at[mine], refl.at[:, here], sems.at[0]),
        copy(far_reflect, refl.at[:, there], sems.at[1]),
        copy(own_courant, cour.at[here], sems.at[2]),
        copy(far_courant, cour.at[there], sems.at[3]),
    ]
    for move in moves:
        move.start()
    wide = band(columns, columns, columns)
    group = down.shape[0]
    tall = band(group, group, rows)
    for i in range(2):
        across[i * columns : (i + 1) * columns] = wide
        down[:, i * group : (i + 1) * group] = tall
    for move in moves:
        move.wait()
    cour[...] = cour[...] * SCALE

    def turn(h, carry):
        for b in range(blocks):
            tile = jnp.concatenate([refl[h, stack * b + i] for i in range(stack)], 0)
            rt[h, b] = tile.astype(F32).T.astype(BF16)
        return carry

    lax.fori_loop(0, offsets, turn, 0)


def vertical(plane_of, z, depth):
    total = EXACT_WEIGHTS[0] * plane_of(z)
    for k in range(1, REACH + 1):
        near = [plane_of(n) for n in (z - k, z + k) if 0 <= n < depth]
        if near:
            total = total + EXACT_WEIGHTS[k] * functools.reduce(jnp.add, near)
    return total


def sideways(terms, across, down):
    n = len(terms)
    group, columns = terms[0].shape
    x_part = jnp.dot(jnp.concatenate(terms, 1), across[0 : n * columns], preferred_element_type=F32)
    y_part = jnp.dot(down[:, 0 : n * group], jnp.concatenate(terms, 0), preferred_element_type=F32)
    return x_part + y_part


def source_of(lag_of, rt, cour, across, down, plain, shifted, turned, source):
    depth, rows, columns = cour.shape
    offsets, blocks = rt.shape[:2]
    group = down.shape[0]
    planes, tiles, stack = group // rows, group // 128, 128 // rows
    for g in range(depth // planes):
        high = jnp.concatenate([plain[g * planes + p].astype(BF16) for p in range(planes)], 0)
        both = sideways([high], across, down)
        for b in range(tiles):
            pieces = []
            for i in range(stack):
                p = b * stack + i
                z = g * planes + p
                upright = vertical(lambda n: plain[n], z, depth)
                pieces.append(cour[z] * (both[p * rows : (p + 1) * rows] + upright))
            shifted[g * tiles + b, LAG : LAG + columns] = jnp.concatenate(pieces, 0).T
    chunk = 64
    for b in range(blocks):
        for r in range(0, columns, chunk):
            total = jnp.zeros((chunk, 128), F32)
            for h in range(offsets):
                image = rt[h, b, r : r + chunk].astype(F32)
                total = total + image * shifted[b, pl.ds(LAG + r - lag_of(h), chunk)]
            turned[b, r : r + chunk] = total
    for b in range(blocks):
        tile = turned[b].T
        for i in range(stack):
            source[stack * b + i] = tile[i * rows : (i + 1) * rows]


def clear_rims(shifted, columns):
    for b in range(shifted.shape[0]):
        shifted[b, 0:LAG] = jnp.zeros((LAG, 128), F32)
        shifted[b, LAG + columns : 2 * LAG + columns] = jnp.zeros((LAG, 128), F32)


def take_field(tests, core, plain):
    for test, at, own, far in tests:
        half = own.shape[1]

        @pl.when(test)
        def _(at=at, own=own, far=far, half=half):
            for z in range(half):
                plain[core * half + z] = own[at, z].astype(F32)
                plain[(1 - core) * half + z] = far[at, z].astype(F32)


def sums_kernel(
    choose, where_ref, owners_ref, lags_ref, rt, cour, across, down, sums, plain, shifted, turned,
):
    first = where_ref[1] * rt.shape[0]
    clear_rims(shifted, cour.shape[2])

    def step(t, carry):
        tests = choose(owners_ref[t] ^ where_ref[0])

        @pl.when(functools.reduce(jnp.logical_or, [test for test, *_ in tests]))
        def _():
            take_field(tests, where_ref[1], plain)
            source_of(lambda h: lags_ref[first + h], rt, cour, across, down, plain, shifted, turned, sums.at[t])

        return carry

    lax.fori_loop(0, ITERS, step, 0)


def steps_kernel(
    choose, where_ref, owners_ref, lags_ref, rt, cour, across, down, kept_ref, given_ref, sums,
    plain, shifted, turned, wave_a, wave_b,
):
    sums_kernel(
        choose, where_ref, owners_ref, lags_ref, rt, cour, across, down, sums, plain, shifted, turned
    )
    depth, rows, _ = cour.shape
    half = depth // 2
    group = down.shape[0]
    planes = group // rows

    def grow(t, now, before):
        for g in range(depth // planes):
            high, low = split(jnp.concatenate([now[g * planes + p] for p in range(planes)], 0))
            both = sideways([high, low], across, down)
            for p in range(planes):
                z = g * planes + p
                laplace = both[p * rows : (p + 1) * rows] + vertical(lambda n: now[n], z, depth)
                before[z] = (2.0 * now[z] - before[z]) + (cour[z] * laplace + sums[t, z])

    wave_a[...] = sums[0]
    wave_b[...] = jnp.zeros(wave_b.shape, F32)

    def pair(i, carry):
        grow(2 * i + 1, wave_a, wave_b)
        grow(2 * i + 2, wave_b, wave_a)
        return carry

    lax.fori_loop(0, (ITERS - 1) // 2, pair, 0)
    last = wave_a
    if ITERS % 2 == 0:
        grow(ITERS - 1, wave_a, wave_b)
        last = wave_b
    core = where_ref[1]
    kept_ref[...] = last[pl.ds(core * half, half)]
    given_ref[...] = last[pl.ds((1 - core) * half, half)]


def swapped(x):
    return lax.ppermute(x, "dep", [(0, 1), (1, 0)])


def flip(x, bits):
    count = lax.axis_size("off")
    return lax.ppermute(x, "off", [(i, i ^ bits) for i in range(count)])


def core_pair(snapshots, reflect, courant, lags, owners):
    count = lax.axis_size("off")
    core = lax.axis_index("dep")
    mine = reflect.shape[0] // 2
    half, rows, columns = courant.shape
    depth = 2 * half
    blocks = depth * rows // 128
    group = 256
    wing = 4
    lines = count // wing
    cut = 2 * (lines - 1) // 3

    z_parts = [flip(snapshots, wing * j) for j in range(1, lines)]
    o_x, o_y = flip(snapshots, 1), flip(snapshots, 2)
    o_d = flip(o_x, 2)
    sent = lax.dynamic_slice_in_dim(reflect, (1 - core) * mine, mine, 0)
    far_reflect = swapped(sent)
    far_courant = swapped(courant)

    smem = pl.BlockSpec(memory_space=pltpu.SMEM)
    anyspace = pl.BlockSpec(memory_space=pl.ANY)
    vmem = pl.BlockSpec(memory_space=pltpu.VMEM)
    where = jnp.stack([lax.axis_index("off"), core]).astype(jnp.int32)
    tables = [
        jax.ShapeDtypeStruct((mine, blocks, columns, 128), BF16),
        jax.ShapeDtypeStruct((depth, rows, columns), F32),
        jax.ShapeDtypeStruct((2 * columns, columns), BF16),
        jax.ShapeDtypeStruct((group, 2 * group), BF16),
    ]
    prepare = pl.pallas_call(
        prepare_kernel,
        out_shape=tables,
        in_specs=[smem] + [anyspace] * 4,
        out_specs=[vmem] * 4,
        scratch_shapes=[
            pltpu.VMEM((mine, depth, rows, columns), BF16),
            pltpu.SemaphoreType.DMA((4,)),
        ],
        compiler_params=pltpu.CompilerParams(vmem_limit_bytes=8 << 20),
        cost_estimate=pl.CostEstimate(flops=10**7, bytes_accessed=6 << 20, transcendentals=0),
    )
    prepared = prepare(where[1:], reflect, far_reflect, courant, far_courant)
    z_all = jnp.concatenate(z_parts, 0)
    z_x, z_y = flip(z_all, 1), flip(z_all, 2)
    d_x = flip(z_x[:cut], 2)
    d_y = flip(z_y[cut:], 1)

    scratch = [
        pltpu.VMEM((depth, rows, columns), F32),
        pltpu.VMEM((blocks, columns + 2 * LAG, 128), F32),
        pltpu.VMEM((blocks, columns, 128), F32),
    ]
    waves = [pltpu.VMEM((depth, rows, columns), F32)] * 2
    params = pltpu.CompilerParams(vmem_limit_bytes=12 << 20)
    cost = pl.CostEstimate(flops=10**9, bytes_accessed=10 << 20, transcendentals=0)
    sums_shape = jax.ShapeDtypeStruct((ITERS, depth, rows, columns), F32)

    def near_banks(owns, fars):
        def choose(apart):
            low, line = apart % wing, apart // wing
            own_line = [((line == 0) & (low == i), 0, owns[i], fars[i]) for i in range(wing)]
            return own_line + [((line > 0) & (low == 0), line - 1, owns[wing], fars[wing])]

        return choose

    def side_banks(owns, fars):
        def choose(apart):
            low, line = apart % wing, apart // wing
            return [((line > 0) & (low == 1 + i), line - 1, owns[i], fars[i]) for i in range(2)]

        return choose

    def far_banks(owns, fars):
        def choose(apart):
            low, line = apart % wing, apart // wing
            return [
                ((low == 3) & (line > 0) & (line <= cut), line - 1, owns[0], fars[0]),
                ((low == 3) & (line > cut), line - 1 - cut, owns[1], fars[1]),
            ]

        return choose

    def run(body, banks, own_parts, extra, out_shape, more_scratch=()):
        far_parts = [swapped(v) for v in own_parts]
        n = len(own_parts)

        def kernel(where_ref, owners_ref, lags_ref, *refs):
            rest = refs[2 * n : 2 * n + 4] + refs[2 * n + 4 + len(extra) :]
            body(banks(refs[:n], refs[n : 2 * n]), where_ref, owners_ref, lags_ref, *rest)

        return pl.pallas_call(
            kernel,
            in_specs=[smem] * 3 + [vmem] * (2 * n + 4 + len(extra)),
            out_shape=out_shape,
            out_specs=[vmem] * len(out_shape),
            scratch_shapes=scratch + list(more_scratch),
            input_output_aliases={3 + 2 * n + 4: len(out_shape) - 1} if extra else {},
            compiler_params=params,
            cost_estimate=cost,
        )(where, owners, lags, *own_parts, *far_parts, *prepared, *extra)

    out_half = jax.ShapeDtypeStruct((half, rows, columns), F32)
    sums = run(sums_kernel, near_banks, [snapshots, o_x, o_y, o_d, z_all], [], [sums_shape])
    sums = run(sums_kernel, side_banks, [z_x, z_y], sums, [sums_shape])
    kept, given, _ = run(steps_kernel, far_banks, [d_x, d_y], sums, [out_half, out_half, sums_shape], waves)

    total = kept + swapped(given)
    pieces = total.reshape(count, half * rows // count, columns)
    summed = lax.all_to_all(pieces, "off", 0, 0).sum(0)
    spread = jnp.broadcast_to(summed[None], pieces.shape)
    return lax.all_to_all(spread, "off", 0, 0).reshape(half, rows, columns)


def solution(mesh):
    offs, deps = mesh.shape["off"], mesh.shape["dep"]

    def per_device(snapshots, reflect, courant, lags, owners):
        fits = (
            deps == 2
            and snapshots.shape[0] == 1
            and offs >= 16
            and offs & (offs - 1) == 0
            and reflect.shape[0] % 2 == 0
            and courant.shape[2] % 128 == 0
            and (courant.shape[0] * courant.shape[1]) % (8 * offs) == 0
            and (courant.shape[0] * courant.shape[1]) % 128 == 0
            and courant.shape[1] % 16 == 0
            and 128 % courant.shape[1] == 0
        )
        body = core_pair if fits else halo_steps
        return body(snapshots, reflect, courant, lags, owners)

    in_specs = (
        P("off", "dep", None, None),
        P("off", "dep", None, None),
        P("dep", None, None),
        P("off"),
        P(),
    )
    return jax.shard_map(
        per_device, mesh=mesh, in_specs=in_specs, out_specs=P("dep", None, None), check_vma=False
    )
```

```python
import functools

import jax
import jax.numpy as jnp
from jax import lax
from jax.experimental import pallas as pl
from jax.experimental.pallas import tpu as pltpu
from jax.sharding import PartitionSpec as P


ITERS = 8
LAG = 32
REACH = 4

STENCIL_WEIGHTS = (-205.0 / 72.0, 8.0 / 5.0, -1.0 / 5.0, 8.0 / 315.0, -1.0 / 560.0)


BF16 = jnp.bfloat16
F32 = jnp.float32


def extended(cells, sides, width):
    for axis, dim in sides:
        count = lax.axis_size(axis)
        ends = count - 1
        head = lax.slice_in_dim(cells, 0, width, axis=dim)
        tail = lax.slice_in_dim(cells, cells.shape[dim] - width, cells.shape[dim], axis=dim)
        cells = jnp.concatenate(
            [
                lax.ppermute(tail, axis, [(i, (i + 1) % count) for i in range(ends)]),
                cells,
                lax.ppermute(head, axis, [((i + 1) % count, i) for i in range(ends)]),
            ],
            axis=dim,
        )
    return cells


def broadcast(x, axis, root):
    mine = lax.axis_index(axis) == root
    return lax.psum(jnp.where(mine, x, jnp.zeros_like(x)), axis)


def stencil(padded, depth_cells, row_cells, column_cells):
    def part(dz, dy, dx):
        return padded[
            4 + dz : 4 + dz + depth_cells, 4 + dy : 4 + dy + row_cells, 4 + dx : 4 + dx + column_cells
        ]

    summed = 3.0 * STENCIL_WEIGHTS[0] * part(0, 0, 0)
    for k in range(1, 5):
        neighbours = part(k, 0, 0) + part(-k, 0, 0)
        neighbours = neighbours + part(0, k, 0) + part(0, -k, 0)
        neighbours = neighbours + part(0, 0, k) + part(0, 0, -k)
        summed = summed + STENCIL_WEIGHTS[k] * neighbours
    return summed


def shifted_sum(reflect, acceleration, lags):
    width_cells = acceleration.shape[2]
    padded = jnp.pad(acceleration, ((0, 0), (0, 0), (LAG, LAG)))

    def add_offset(offset_index, summed):
        lag_now = lags[offset_index]
        window = lax.dynamic_slice_in_dim(padded, LAG - lag_now, width_cells, 2)
        return summed + reflect[offset_index].astype(F32) * window

    return lax.fori_loop(0, reflect.shape[0], add_offset, jnp.zeros(acceleration.shape, F32))


def halo_steps(snapshots, reflect, courant, lags, owners):
    own_layers = extended(snapshots[0], (("dep", 0),), 4)
    own_ready = courant * stencil(
        jnp.pad(own_layers, ((0, 0), (4, 4), (4, 4))).astype(F32), *courant.shape
    )
    scattered = jnp.zeros(courant.shape, F32)
    previous = jnp.zeros(courant.shape, F32)
    for step_now in range(ITERS):
        acceleration = broadcast(own_ready, "off", owners[step_now])
        source = shifted_sum(reflect, acceleration, lags)
        field = jnp.pad(extended(scattered, (("dep", 0),), 4), ((0, 0), (4, 4), (4, 4)))
        updated = 2.0 * scattered - previous + courant * stencil(field, *courant.shape) + source
        previous = scattered
        scattered = updated
    return lax.psum(scattered, "off")


def split(v):
    high = v.astype(BF16)
    return high, (v - high.astype(F32)).astype(BF16)


EXACT_WEIGHTS = tuple(w / 4096.0 for w in (-43050.0, 8064.0, -1008.0, 128.0, -9.0))
SCALE = 4096.0 / 5040.0


def band(rows, columns, block):
    i = lax.broadcasted_iota(jnp.int32, (rows, columns), 0)
    j = lax.broadcasted_iota(jnp.int32, (rows, columns), 1)
    apart = jnp.where(i // block == j // block, jnp.abs(i - j), 0)
    full = jnp.zeros((rows, columns), F32)
    for k in range(1, REACH + 1):
        full = jnp.where(apart == k, EXACT_WEIGHTS[k], full)
    return full.astype(BF16)


def prepare_kernel(core_ref, own_reflect, far_reflect, own_courant, far_courant, rt, cour, across, down):
    core = core_ref[0]
    half, rows, columns = own_courant.shape
    offsets, blocks = rt.shape[:2]
    stack = 128 // rows
    here, there = core * half, (1 - core) * half
    wide = band(columns, columns, columns)
    group = down.shape[0]
    tall = band(group, group, rows)
    for i in range(2):
        across[i * columns : (i + 1) * columns] = wide
        down[:, i * group : (i + 1) * group] = tall
    cour[pl.ds(here, half)] = own_courant[...]
    cour[pl.ds(there, half)] = far_courant[...]

    def turn(h, carry):
        for source, start in ((own_reflect, here // stack), (far_reflect, there // stack)):
            for b in range(blocks // 2):
                tile = jnp.concatenate([source[h, stack * b + i] for i in range(stack)], 0)
                rt[h, start + b] = tile.astype(F32).T.astype(BF16)
        return carry

    lax.fori_loop(0, offsets, turn, 0)


def vertical(plane_of, z, depth):
    total = EXACT_WEIGHTS[0] * plane_of(z)
    for k in range(1, REACH + 1):
        near = [plane_of(n) for n in (z - k, z + k) if 0 <= n < depth]
        if near:
            total = total + EXACT_WEIGHTS[k] * functools.reduce(jnp.add, near)
    return total


def sideways(terms, across, down):
    n = len(terms)
    group, columns = terms[0].shape
    x_part = jnp.dot(jnp.concatenate(terms, 1), across[0 : n * columns], preferred_element_type=F32)
    y_part = jnp.dot(down[:, 0 : n * group], jnp.concatenate(terms, 0), preferred_element_type=F32)
    return x_part + y_part


def source_of(lag_of, rt, cour, across, down, plain, shifted, turned, source):
    depth, rows, columns = cour.shape
    offsets, blocks = rt.shape[:2]
    group = down.shape[0]
    planes, tiles, stack = group // rows, group // 128, 128 // rows
    for g in range(depth // planes):
        high = jnp.concatenate([plain[g * planes + p].astype(BF16) for p in range(planes)], 0)
        both = sideways([high], across, down)
        for b in range(tiles):
            pieces = []
            for i in range(stack):
                p = b * stack + i
                z = g * planes + p
                upright = vertical(lambda n: plain[n], z, depth)
                pieces.append(cour[z] * (both[p * rows : (p + 1) * rows] + upright))
            shifted[g * tiles + b, LAG : LAG + columns] = jnp.concatenate(pieces, 0).T
    chunk = 64
    for b in range(blocks):
        for r in range(0, columns, chunk):
            total = jnp.zeros((chunk, 128), F32)
            for h in range(offsets):
                image = rt[h, b, r : r + chunk].astype(F32)
                total = total + image * shifted[b, pl.ds(LAG + r - lag_of(h), chunk)]
            turned[b, r : r + chunk] = total
    for b in range(blocks):
        tile = turned[b].T
        for i in range(stack):
            source[stack * b + i] = tile[i * rows : (i + 1) * rows]


def clear_rims(shifted, columns):
    for b in range(shifted.shape[0]):
        shifted[b, 0:LAG] = jnp.zeros((LAG, 128), F32)
        shifted[b, LAG + columns : 2 * LAG + columns] = jnp.zeros((LAG, 128), F32)


def join_kernel(*refs):
    *parts, out = refs
    for i, part in enumerate(parts):
        out[i] = part[0]


def pick_kernel(core_ref, first, second, out):
    for i, part in enumerate((first, second)):

        @pl.when(core_ref[0] == i)
        def _(part=part):
            out[...] = part[...]


def take_field(tests, core, plain):
    for test, at, own, far in tests:
        half = own.shape[1]

        @pl.when(test)
        def _(at=at, own=own, far=far, half=half):
            for z in range(half):
                plain[core * half + z] = own[at, z].astype(F32)
                plain[(1 - core) * half + z] = far[at, z].astype(F32)


def sums_kernel(
    choose, where_ref, owners_ref, lags_ref, rt, cour, across, down, sums, plain, shifted, turned,
):
    first = where_ref[1] * rt.shape[0]
    clear_rims(shifted, cour.shape[2])

    def step(t, carry):
        tests = choose(owners_ref[t] ^ where_ref[0])

        @pl.when(functools.reduce(jnp.logical_or, [test for test, *_ in tests]))
        def _():
            take_field(tests, where_ref[1], plain)
            source_of(lambda h: lags_ref[first + h], rt, cour, across, down, plain, shifted, turned, sums.at[t])

        return carry

    lax.fori_loop(0, ITERS, step, 0)


def steps_kernel(
    choose, where_ref, owners_ref, lags_ref, rt, cour, across, down, kept_ref, given_ref, sums,
    plain, shifted, turned, wave_a, wave_b,
):
    sums_kernel(
        choose, where_ref, owners_ref, lags_ref, rt, cour, across, down, sums, plain, shifted, turned
    )
    depth, rows, _ = cour.shape
    half = depth // 2
    group = down.shape[0]
    planes = group // rows

    def grow(t, now, before):
        for g in range(depth // planes):
            high, low = split(jnp.concatenate([now[g * planes + p] for p in range(planes)], 0))
            both = sideways([high, low], across, down)
            for p in range(planes):
                z = g * planes + p
                laplace = both[p * rows : (p + 1) * rows] + vertical(lambda n: now[n], z, depth)
                before[z] = (2.0 * now[z] - before[z]) + (cour[z] * laplace + sums[t, z])

    wave_a[...] = sums[0]
    wave_b[...] = jnp.zeros(wave_b.shape, F32)

    def pair(i, carry):
        grow(2 * i + 1, wave_a, wave_b)
        grow(2 * i + 2, wave_b, wave_a)
        return carry

    lax.fori_loop(0, (ITERS - 1) // 2, pair, 0)
    last = wave_a
    if ITERS % 2 == 0:
        grow(ITERS - 1, wave_a, wave_b)
        last = wave_b
    core = where_ref[1]
    kept_ref[...] = last[pl.ds(core * half, half)]
    given_ref[...] = last[pl.ds((1 - core) * half, half)]


def swapped(x):
    return lax.ppermute(x, "dep", [(0, 1), (1, 0)])


def flip(x, bits):
    count = lax.axis_size("off")
    return lax.ppermute(x, "off", [(i, i ^ bits) for i in range(count)])


def cross(x):
    count = lax.axis_size("off")
    pairs = [(2 * i + c, 2 * (i ^ (2 - c)) + c) for i in range(count) for c in range(2)]
    return lax.ppermute(x, ("off", "dep"), pairs)


def core_pair(snapshots, reflect, courant, lags, owners):
    count = lax.axis_size("off")
    core = lax.axis_index("dep")
    mine = reflect.shape[0] // 2
    half, rows, columns = courant.shape
    depth = 2 * half
    blocks = depth * rows // 128
    group = 256
    wing = 4
    lines = count // wing

    z_parts = [flip(snapshots, wing * j) for j in range(1, lines)]
    o_x, o_y = flip(snapshots, 1), flip(snapshots, 2)
    o_d = flip(o_x, 2)
    sent = lax.dynamic_slice_in_dim(reflect, (1 - core) * mine, mine, 0)
    far_reflect = swapped(sent)
    own_reflect = lax.dynamic_slice_in_dim(reflect, core * mine, mine, 0)
    own_courant = courant * SCALE
    far_courant = swapped(own_courant)

    smem = pl.BlockSpec(memory_space=pltpu.SMEM)
    anyspace = pl.BlockSpec(memory_space=pl.ANY)
    vmem = pl.BlockSpec(memory_space=pltpu.VMEM)
    where = jnp.stack([lax.axis_index("off"), core]).astype(jnp.int32)
    tables = [
        jax.ShapeDtypeStruct((mine, blocks, columns, 128), BF16),
        jax.ShapeDtypeStruct((depth, rows, columns), F32),
        jax.ShapeDtypeStruct((2 * columns, columns), BF16),
        jax.ShapeDtypeStruct((group, 2 * group), BF16),
    ]
    prepare = pl.pallas_call(
        prepare_kernel,
        out_shape=tables,
        in_specs=[smem] + [vmem] * 4,
        out_specs=[vmem] * 4,
        compiler_params=pltpu.CompilerParams(vmem_limit_bytes=8 << 20),
        cost_estimate=pl.CostEstimate(flops=10**7, bytes_accessed=6 << 20, transcendentals=0),
    )
    prepared = prepare(where[1:], own_reflect, far_reflect, own_courant, far_courant)
    z_shape = jax.ShapeDtypeStruct((lines - 1, half, rows, columns), BF16)
    small = pl.CostEstimate(flops=0, bytes_accessed=1 << 20, transcendentals=0)
    join = pl.pallas_call(
        join_kernel,
        out_shape=z_shape,
        in_specs=[vmem] * (lines - 1),
        out_specs=vmem,
        compiler_params=pltpu.CompilerParams(vmem_limit_bytes=4 << 20),
        cost_estimate=small,
    )
    pick = pl.pallas_call(
        pick_kernel,
        out_shape=z_shape,
        in_specs=[smem, vmem, vmem],
        out_specs=vmem,
        compiler_params=pltpu.CompilerParams(vmem_limit_bytes=4 << 20),
        cost_estimate=small,
    )
    z_all = join(*z_parts)
    z_x, z_y = flip(z_all, 1), flip(z_all, 2)
    picked = pick(where[1:], z_x, z_y)
    diagonal = cross(picked)

    scratch = [
        pltpu.VMEM((depth, rows, columns), F32),
        pltpu.VMEM((blocks, columns + 2 * LAG, 128), F32),
        pltpu.VMEM((blocks, columns, 128), F32),
    ]
    waves = [pltpu.VMEM((depth, rows, columns), F32)] * 2
    params = pltpu.CompilerParams(vmem_limit_bytes=12 << 20)
    cost = pl.CostEstimate(flops=10**9, bytes_accessed=10 << 20, transcendentals=0)
    sums_shape = jax.ShapeDtypeStruct((ITERS, depth, rows, columns), F32)

    def near_banks(owns, fars):
        def choose(apart):
            low, line = apart % wing, apart // wing
            own_line = [((line == 0) & (low == i), 0, owns[i], fars[i]) for i in range(wing)]
            return own_line + [((line > 0) & (low == 0), line - 1, owns[wing], fars[wing])]

        return choose

    def side_banks(owns, fars):
        def choose(apart):
            low, line = apart % wing, apart // wing
            return [((line > 0) & (low == 1 + i), line - 1, owns[i], fars[i]) for i in range(2)]

        return choose

    def far_banks(owns, fars):
        def choose(apart):
            low, line = apart % wing, apart // wing
            return [((low == 3) & (line > 0), line - 1, owns[0], fars[0])]

        return choose

    def run(body, banks, own_parts, extra, out_shape, more_scratch=()):
        far_parts = [swapped(v) for v in own_parts]
        n = len(own_parts)

        def kernel(where_ref, owners_ref, lags_ref, *refs):
            rest = refs[2 * n : 2 * n + 4] + refs[2 * n + 4 + len(extra) :]
            body(banks(refs[:n], refs[n : 2 * n]), where_ref, owners_ref, lags_ref, *rest)

        return pl.pallas_call(
            kernel,
            in_specs=[smem] * 3 + [vmem] * (2 * n + 4 + len(extra)),
            out_shape=out_shape,
            out_specs=[vmem] * len(out_shape),
            scratch_shapes=scratch + list(more_scratch),
            input_output_aliases={3 + 2 * n + 4: len(out_shape) - 1} if extra else {},
            compiler_params=params,
            cost_estimate=cost,
        )(where, owners, lags, *own_parts, *far_parts, *prepared, *extra)

    out_half = jax.ShapeDtypeStruct((half, rows, columns), F32)
    sums = run(sums_kernel, near_banks, [snapshots, o_x, o_y, o_d, z_all], [], [sums_shape])
    sums = run(sums_kernel, side_banks, [z_x, z_y], sums, [sums_shape])
    kept, given, _ = run(steps_kernel, far_banks, [diagonal], sums, [out_half, out_half, sums_shape], waves)

    total = kept + swapped(given)
    pieces = total.reshape(count, half * rows // count, columns)
    summed = lax.all_to_all(pieces, "off", 0, 0).sum(0)
    spread = jnp.broadcast_to(summed[None], pieces.shape)
    return lax.all_to_all(spread, "off", 0, 0).reshape(half, rows, columns)


def solution(mesh):
    offs, deps = mesh.shape["off"], mesh.shape["dep"]

    def per_device(snapshots, reflect, courant, lags, owners):
        fits = (
            deps == 2
            and snapshots.shape[0] == 1
            and offs >= 16
            and offs & (offs - 1) == 0
            and reflect.shape[0] % 2 == 0
            and courant.shape[2] % 128 == 0
            and (courant.shape[0] * courant.shape[1]) % (8 * offs) == 0
            and (courant.shape[0] * courant.shape[1]) % 128 == 0
            and courant.shape[1] % 16 == 0
            and 128 % courant.shape[1] == 0
        )
        body = core_pair if fits else halo_steps
        return body(snapshots, reflect, courant, lags, owners)

    in_specs = (
        P("off", "dep", None, None),
        P("off", "dep", None, None),
        P("dep", None, None),
        P("off"),
        P(),
    )
    return jax.shard_map(
        per_device, mesh=mesh, in_specs=in_specs, out_specs=P("dep", None, None), check_vma=False
    )
```

```python
import functools

import jax
import jax.numpy as jnp
from jax import lax
from jax.experimental import pallas as pl
from jax.experimental.pallas import tpu as pltpu
from jax.sharding import PartitionSpec as P


ITERS = 8
LAG = 32
REACH = 4

STENCIL_WEIGHTS = (-205.0 / 72.0, 8.0 / 5.0, -1.0 / 5.0, 8.0 / 315.0, -1.0 / 560.0)


BF16 = jnp.bfloat16
F32 = jnp.float32


def extended(cells, sides, width):
    for axis, dim in sides:
        count = lax.axis_size(axis)
        ends = count - 1
        head = lax.slice_in_dim(cells, 0, width, axis=dim)
        tail = lax.slice_in_dim(cells, cells.shape[dim] - width, cells.shape[dim], axis=dim)
        cells = jnp.concatenate(
            [
                lax.ppermute(tail, axis, [(i, (i + 1) % count) for i in range(ends)]),
                cells,
                lax.ppermute(head, axis, [((i + 1) % count, i) for i in range(ends)]),
            ],
            axis=dim,
        )
    return cells


def broadcast(x, axis, root):
    mine = lax.axis_index(axis) == root
    return lax.psum(jnp.where(mine, x, jnp.zeros_like(x)), axis)


def stencil(padded, depth_cells, row_cells, column_cells):
    def part(dz, dy, dx):
        return padded[
            4 + dz : 4 + dz + depth_cells, 4 + dy : 4 + dy + row_cells, 4 + dx : 4 + dx + column_cells
        ]

    summed = 3.0 * STENCIL_WEIGHTS[0] * part(0, 0, 0)
    for k in range(1, 5):
        neighbours = part(k, 0, 0) + part(-k, 0, 0)
        neighbours = neighbours + part(0, k, 0) + part(0, -k, 0)
        neighbours = neighbours + part(0, 0, k) + part(0, 0, -k)
        summed = summed + STENCIL_WEIGHTS[k] * neighbours
    return summed


def shifted_sum(reflect, acceleration, lags):
    width_cells = acceleration.shape[2]
    padded = jnp.pad(acceleration, ((0, 0), (0, 0), (LAG, LAG)))

    def add_offset(offset_index, summed):
        lag_now = lags[offset_index]
        window = lax.dynamic_slice_in_dim(padded, LAG - lag_now, width_cells, 2)
        return summed + reflect[offset_index].astype(F32) * window

    return lax.fori_loop(0, reflect.shape[0], add_offset, jnp.zeros(acceleration.shape, F32))


def halo_steps(snapshots, reflect, courant, lags, owners):
    own_layers = extended(snapshots[0], (("dep", 0),), 4)
    own_ready = courant * stencil(
        jnp.pad(own_layers, ((0, 0), (4, 4), (4, 4))).astype(F32), *courant.shape
    )
    scattered = jnp.zeros(courant.shape, F32)
    previous = jnp.zeros(courant.shape, F32)
    for step_now in range(ITERS):
        acceleration = broadcast(own_ready, "off", owners[step_now])
        source = shifted_sum(reflect, acceleration, lags)
        field = jnp.pad(extended(scattered, (("dep", 0),), 4), ((0, 0), (4, 4), (4, 4)))
        updated = 2.0 * scattered - previous + courant * stencil(field, *courant.shape) + source
        previous = scattered
        scattered = updated
    return lax.psum(scattered, "off")


def split(v):
    high = v.astype(BF16)
    return high, (v - high.astype(F32)).astype(BF16)


EXACT_WEIGHTS = tuple(w / 4096.0 for w in (-43050.0, 8064.0, -1008.0, 128.0, -9.0))
SCALE = 4096.0 / 5040.0


def band(rows, columns, block):
    i = lax.broadcasted_iota(jnp.int32, (rows, columns), 0)
    j = lax.broadcasted_iota(jnp.int32, (rows, columns), 1)
    apart = jnp.where(i // block == j // block, jnp.abs(i - j), 0)
    full = jnp.zeros((rows, columns), F32)
    for k in range(1, REACH + 1):
        full = jnp.where(apart == k, EXACT_WEIGHTS[k], full)
    return full.astype(BF16)


def prepare_kernel(own_reflect, far_reflect, own_courant, far_courant, rt, cour, across, down):
    core = lax.axis_index("dep")
    half, rows, columns = own_courant.shape
    offsets, blocks = rt.shape[:2]
    stack = 128 // rows
    here, there = core * half, (1 - core) * half
    wide = band(columns, columns, columns)
    group = down.shape[0]
    tall = band(group, group, rows)
    for i in range(2):
        across[i * columns : (i + 1) * columns] = wide
        down[:, i * group : (i + 1) * group] = tall
    cour[pl.ds(here, half)] = own_courant[...]
    cour[pl.ds(there, half)] = far_courant[...]

    def turn(h, carry):
        for source, start in ((own_reflect, here // stack), (far_reflect, there // stack)):
            for b in range(blocks // 2):
                tile = jnp.concatenate([source[h, stack * b + i] for i in range(stack)], 0)
                rt[h, start + b] = tile.astype(F32).T.astype(BF16)
        return carry

    lax.fori_loop(0, offsets, turn, 0)


def vertical(plane_of, z, depth):
    total = EXACT_WEIGHTS[0] * plane_of(z)
    for k in range(1, REACH + 1):
        near = [plane_of(n) for n in (z - k, z + k) if 0 <= n < depth]
        if near:
            total = total + EXACT_WEIGHTS[k] * functools.reduce(jnp.add, near)
    return total


def sideways(terms, across, down):
    n = len(terms)
    group, columns = terms[0].shape
    x_part = jnp.dot(jnp.concatenate(terms, 1), across[0 : n * columns], preferred_element_type=F32)
    y_part = jnp.dot(down[:, 0 : n * group], jnp.concatenate(terms, 0), preferred_element_type=F32)
    return x_part + y_part


def source_of(lag_of, rt, cour, across, down, plain, shifted, turned, source):
    depth, rows, columns = cour.shape
    offsets, blocks = rt.shape[:2]
    group = down.shape[0]
    planes, tiles, stack = group // rows, group // 128, 128 // rows
    for g in range(depth // planes):
        high = jnp.concatenate([plain[g * planes + p].astype(BF16) for p in range(planes)], 0)
        both = sideways([high], across, down)
        for b in range(tiles):
            pieces = []
            for i in range(stack):
                p = b * stack + i
                z = g * planes + p
                upright = vertical(lambda n: plain[n], z, depth)
                pieces.append(cour[z] * (both[p * rows : (p + 1) * rows] + upright))
            shifted[g * tiles + b, LAG : LAG + columns] = jnp.concatenate(pieces, 0).T
    chunk = 64
    for b in range(blocks):
        for r in range(0, columns, chunk):
            total = jnp.zeros((chunk, 128), F32)
            for h in range(offsets):
                image = rt[h, b, r : r + chunk].astype(F32)
                total = total + image * shifted[b, pl.ds(LAG + r - lag_of(h), chunk)]
            turned[b, r : r + chunk] = total
    for b in range(blocks):
        tile = turned[b].T
        for i in range(stack):
            source[stack * b + i] = tile[i * rows : (i + 1) * rows]


def clear_rims(shifted, columns):
    for b in range(shifted.shape[0]):
        shifted[b, 0:LAG] = jnp.zeros((LAG, 128), F32)
        shifted[b, LAG + columns : 2 * LAG + columns] = jnp.zeros((LAG, 128), F32)


def join_kernel(*refs):
    *parts, out = refs
    for i, part in enumerate(parts):
        out[i] = part[0]


def take_field(tests, core, plain):
    for test, at, own, far in tests:
        half = own.shape[1]

        @pl.when(test)
        def _(at=at, own=own, far=far, half=half):
            for z in range(half):
                plain[core * half + z] = own[at, z].astype(F32)
                plain[(1 - core) * half + z] = far[at, z].astype(F32)


def sums_kernel(groups, where_now, owners_ref, lags_ref, rt, cour, across, down, sums, plain, shifted, turned):
    first = where_now[1] * rt.shape[0]
    clear_rims(shifted, cour.shape[2])

    def any_of(tests):
        return functools.reduce(jnp.logical_or, [test for test, *_ in tests])

    def step(t, counts):
        taken, after = [], []
        for (choose, low, high), count in zip(groups, counts, strict=True):
            tests = choose(owners_ref[t] ^ where_now[0])
            due = (count >= low) & (count < high)
            taken += [(test & due, *bank) for test, *bank in tests]
            after.append(count + any_of(tests).astype(jnp.int32))

        @pl.when(any_of(taken))
        def _():
            take_field(taken, where_now[1], plain)
            source_of(lambda h: lags_ref[first + h], rt, cour, across, down, plain, shifted, turned, sums.at[t])

        return tuple(after)

    lax.fori_loop(0, ITERS, step, tuple(jnp.int32(0) for _ in groups))


def steps_kernel(
    groups, where_now, owners_ref, lags_ref, rt, cour, across, down, kept_ref, given_ref, sums,
    plain, shifted, turned, wave_a, wave_b,
):
    sums_kernel(
        groups, where_now, owners_ref, lags_ref, rt, cour, across, down, sums, plain, shifted, turned
    )
    depth, rows, _ = cour.shape
    half = depth // 2
    group = down.shape[0]
    planes = group // rows

    def grow(t, now, before):
        for g in range(depth // planes):
            high, low = split(jnp.concatenate([now[g * planes + p] for p in range(planes)], 0))
            both = sideways([high, low], across, down)
            for p in range(planes):
                z = g * planes + p
                laplace = both[p * rows : (p + 1) * rows] + vertical(lambda n: now[n], z, depth)
                before[z] = (2.0 * now[z] - before[z]) + (cour[z] * laplace + sums[t, z])

    wave_a[...] = sums[0]
    wave_b[...] = jnp.zeros(wave_b.shape, F32)

    def pair(i, carry):
        grow(2 * i + 1, wave_a, wave_b)
        grow(2 * i + 2, wave_b, wave_a)
        return carry

    lax.fori_loop(0, (ITERS - 1) // 2, pair, 0)
    last = wave_a
    if ITERS % 2 == 0:
        grow(ITERS - 1, wave_a, wave_b)
        last = wave_b
    core = where_now[1]
    kept_ref[...] = last[pl.ds(core * half, half)]
    given_ref[...] = last[pl.ds((1 - core) * half, half)]


def swapped(x):
    return lax.ppermute(x, "dep", [(0, 1), (1, 0)])


def flip(x, bits):
    count = lax.axis_size("off")
    return lax.ppermute(x, "off", [(i, i ^ bits) for i in range(count)])


def core_pair(snapshots, reflect, courant, lags, owners):
    count = lax.axis_size("off")
    core = lax.axis_index("dep")
    mine = reflect.shape[0] // 2
    half, rows, columns = courant.shape
    depth = 2 * half
    blocks = depth * rows // 128
    group = 256
    wing = 4
    lines = count // wing

    z_parts = [flip(snapshots, wing * j) for j in range(1, lines)]
    o_x, o_y = flip(snapshots, 1), flip(snapshots, 2)
    o_d = flip(o_x, 2)
    sent = lax.dynamic_slice_in_dim(reflect, (1 - core) * mine, mine, 0)
    far_reflect = swapped(sent)
    own_reflect = lax.dynamic_slice_in_dim(reflect, core * mine, mine, 0)
    own_courant = courant * SCALE
    far_courant = swapped(own_courant)

    smem = pl.BlockSpec(memory_space=pltpu.SMEM)
    anyspace = pl.BlockSpec(memory_space=pl.ANY)
    vmem = pl.BlockSpec(memory_space=pltpu.VMEM)
    tables = [
        jax.ShapeDtypeStruct((mine, blocks, columns, 128), BF16),
        jax.ShapeDtypeStruct((depth, rows, columns), F32),
        jax.ShapeDtypeStruct((2 * columns, columns), BF16),
        jax.ShapeDtypeStruct((group, 2 * group), BF16),
    ]
    prepare = pl.pallas_call(
        prepare_kernel,
        out_shape=tables,
        in_specs=[vmem] * 4,
        out_specs=[vmem] * 4,
        compiler_params=pltpu.CompilerParams(vmem_limit_bytes=6 << 20),
        cost_estimate=pl.CostEstimate(flops=10**7, bytes_accessed=6 << 20, transcendentals=0),
    )
    prepared = prepare(own_reflect, far_reflect, own_courant, far_courant)
    z_shape = jax.ShapeDtypeStruct((lines - 1, half, rows, columns), BF16)
    small = pl.CostEstimate(flops=0, bytes_accessed=1 << 20, transcendentals=0)
    join = pl.pallas_call(
        join_kernel,
        out_shape=z_shape,
        in_specs=[vmem] * (lines - 1),
        out_specs=vmem,
        compiler_params=pltpu.CompilerParams(vmem_limit_bytes=2 << 20),
        cost_estimate=small,
    )
    z_all = join(*z_parts)
    z_x, z_y = flip(z_all, 1), flip(z_all, 2)
    d_parts = [flip(o_d, wing * j) for j in range(1, lines)]
    d_all = join(*d_parts)

    scratch = [
        pltpu.VMEM((depth, rows, columns), F32),
        pltpu.VMEM((blocks, columns + 2 * LAG, 128), F32),
        pltpu.VMEM((blocks, columns, 128), F32),
    ]
    waves = [pltpu.VMEM((depth, rows, columns), F32)] * 2
    params = pltpu.CompilerParams(vmem_limit_bytes=6 << 20)
    cost = pl.CostEstimate(flops=10**9, bytes_accessed=10 << 20, transcendentals=0)
    sums_shape = jax.ShapeDtypeStruct((ITERS, depth, rows, columns), F32)

    def near_banks(owns, fars):
        def choose(apart):
            low, line = apart % wing, apart // wing
            own_line = [((line == 0) & (low == i), 0, owns[i], fars[i]) for i in range(wing)]
            return own_line + [((line > 0) & (low == 0), line - 1, owns[wing], fars[wing])]

        return choose

    def side_banks(owns, fars):
        def choose(apart):
            low, line = apart % wing, apart // wing
            return [((line > 0) & (low == 1 + i), line - 1, owns[i], fars[i]) for i in range(2)]

        return choose

    def far_banks(owns, fars):
        def choose(apart):
            low, line = apart % wing, apart // wing
            return [((low == 3) & (line > 0), line - 1, owns[0], fars[0])]

        return choose

    def both_halves(own_parts):
        return own_parts, [swapped(v) for v in own_parts]

    def run(body, groups, extra, out_shape, more_scratch=()):
        arrays = [v for (owns, fars), *_ in groups for v in [*owns, *fars]]
        n = len(arrays)

        def kernel(owners_ref, lags_ref, *refs):
            where_now = lax.axis_index("off"), lax.axis_index("dep")
            given, chosen = list(refs[:n]), []
            for (owns, fars), banks, low, high in groups:
                own_refs = [given.pop(0) for _ in owns]
                far_refs = [given.pop(0) for _ in fars]
                chosen.append((banks(own_refs, far_refs), low, high))
            rest = refs[n : n + 4] + refs[n + 4 + len(extra) :]
            body(chosen, where_now, owners_ref, lags_ref, *rest)

        return pl.pallas_call(
            kernel,
            in_specs=[smem] * 2 + [vmem] * (n + 4 + len(extra)),
            out_shape=out_shape,
            out_specs=[vmem] * len(out_shape),
            scratch_shapes=scratch + list(more_scratch),
            input_output_aliases={2 + n + 4: len(out_shape) - 1} if extra else {},
            compiler_params=params,
            cost_estimate=cost,
        )(owners, lags, *arrays, *prepared, *extra)

    out_half = jax.ShapeDtypeStruct((half, rows, columns), F32)
    near = both_halves([snapshots, o_x, o_y, o_d, z_all])
    side = both_halves([z_x, z_y])
    far = both_halves([d_all])
    sums = run(sums_kernel, [(near, near_banks, 0, ITERS)], [], [sums_shape])
    sums = run(sums_kernel, [(side, side_banks, 0, ITERS)], sums, [sums_shape])
    groups = [(far, far_banks, 0, ITERS)]
    kept, given, _ = run(steps_kernel, groups, sums, [out_half, out_half, sums_shape], waves)

    total = kept + swapped(given)
    pieces = total.reshape(count, half * rows // count, columns)
    summed = lax.all_to_all(pieces, "off", 0, 0).sum(0)
    spread = jnp.broadcast_to(summed[None], pieces.shape)
    return lax.all_to_all(spread, "off", 0, 0).reshape(half, rows, columns)


def solution(mesh):
    offs, deps = mesh.shape["off"], mesh.shape["dep"]

    def per_device(snapshots, reflect, courant, lags, owners):
        fits = (
            deps == 2
            and snapshots.shape[0] == 1
            and offs >= 16
            and offs & (offs - 1) == 0
            and reflect.shape[0] % 2 == 0
            and courant.shape[2] % 128 == 0
            and (courant.shape[0] * courant.shape[1]) % (8 * offs) == 0
            and (courant.shape[0] * courant.shape[1]) % 128 == 0
            and courant.shape[1] % 16 == 0
            and 128 % courant.shape[1] == 0
        )
        body = core_pair if fits else halo_steps
        return body(snapshots, reflect, courant, lags, owners)

    in_specs = (
        P("off", "dep", None, None),
        P("off", "dep", None, None),
        P("dep", None, None),
        P("off"),
        P(),
    )
    return jax.shard_map(
        per_device, mesh=mesh, in_specs=in_specs, out_specs=P("dep", None, None), check_vma=False
    )
```

```python
import functools

import jax
import jax.numpy as jnp
from jax import lax
from jax.experimental import pallas as pl
from jax.experimental.pallas import tpu as pltpu
from jax.sharding import PartitionSpec as P


ITERS = 8
LAG = 32
REACH = 4

STENCIL_WEIGHTS = (-205.0 / 72.0, 8.0 / 5.0, -1.0 / 5.0, 8.0 / 315.0, -1.0 / 560.0)


BF16 = jnp.bfloat16
F32 = jnp.float32


def extended(cells, sides, width):
    for axis, dim in sides:
        count = lax.axis_size(axis)
        ends = count - 1
        head = lax.slice_in_dim(cells, 0, width, axis=dim)
        tail = lax.slice_in_dim(cells, cells.shape[dim] - width, cells.shape[dim], axis=dim)
        cells = jnp.concatenate(
            [
                lax.ppermute(tail, axis, [(i, (i + 1) % count) for i in range(ends)]),
                cells,
                lax.ppermute(head, axis, [((i + 1) % count, i) for i in range(ends)]),
            ],
            axis=dim,
        )
    return cells


def broadcast(x, axis, root):
    mine = lax.axis_index(axis) == root
    return lax.psum(jnp.where(mine, x, jnp.zeros_like(x)), axis)


def stencil(padded, depth_cells, row_cells, column_cells):
    def part(dz, dy, dx):
        return padded[
            4 + dz : 4 + dz + depth_cells, 4 + dy : 4 + dy + row_cells, 4 + dx : 4 + dx + column_cells
        ]

    summed = 3.0 * STENCIL_WEIGHTS[0] * part(0, 0, 0)
    for k in range(1, 5):
        neighbours = part(k, 0, 0) + part(-k, 0, 0)
        neighbours = neighbours + part(0, k, 0) + part(0, -k, 0)
        neighbours = neighbours + part(0, 0, k) + part(0, 0, -k)
        summed = summed + STENCIL_WEIGHTS[k] * neighbours
    return summed


def shifted_sum(reflect, acceleration, lags):
    width_cells = acceleration.shape[2]
    padded = jnp.pad(acceleration, ((0, 0), (0, 0), (LAG, LAG)))

    def add_offset(offset_index, summed):
        lag_now = lags[offset_index]
        window = lax.dynamic_slice_in_dim(padded, LAG - lag_now, width_cells, 2)
        return summed + reflect[offset_index].astype(F32) * window

    return lax.fori_loop(0, reflect.shape[0], add_offset, jnp.zeros(acceleration.shape, F32))


def halo_steps(snapshots, reflect, courant, lags, owners):
    own_layers = extended(snapshots[0], (("dep", 0),), 4)
    own_ready = courant * stencil(
        jnp.pad(own_layers, ((0, 0), (4, 4), (4, 4))).astype(F32), *courant.shape
    )
    scattered = jnp.zeros(courant.shape, F32)
    previous = jnp.zeros(courant.shape, F32)
    for step_now in range(ITERS):
        acceleration = broadcast(own_ready, "off", owners[step_now])
        source = shifted_sum(reflect, acceleration, lags)
        field = jnp.pad(extended(scattered, (("dep", 0),), 4), ((0, 0), (4, 4), (4, 4)))
        updated = 2.0 * scattered - previous + courant * stencil(field, *courant.shape) + source
        previous = scattered
        scattered = updated
    return lax.psum(scattered, "off")


def split(v):
    high = v.astype(BF16)
    return high, (v - high.astype(F32)).astype(BF16)


EXACT_WEIGHTS = tuple(w / 4096.0 for w in (-43050.0, 8064.0, -1008.0, 128.0, -9.0))
SCALE = 4096.0 / 5040.0


def band(rows, columns, block):
    i = lax.broadcasted_iota(jnp.int32, (rows, columns), 0)
    j = lax.broadcasted_iota(jnp.int32, (rows, columns), 1)
    blocks_apart, cells_apart = jnp.abs(i // block - j // block), jnp.abs(i % block - j % block)
    apart = jnp.where(blocks_apart == 0, cells_apart, jnp.where(cells_apart == 0, blocks_apart, 0))
    full = jnp.zeros((rows, columns), F32)
    for k in range(1, REACH + 1):
        full = jnp.where(apart == k, EXACT_WEIGHTS[k], full)
    return full.astype(BF16)


def prepare_kernel(own_reflect, far_reflect, own_courant, far_courant, rt, cour, across, down):
    core = lax.axis_index("dep")
    half, rows, columns = own_courant.shape
    offsets, blocks = rt.shape[:2]
    stack = 128 // rows
    here, there = core * half, (1 - core) * half
    wide = band(columns, columns, columns)
    group = down.shape[0]
    tall = band(group, group, rows)
    for i in range(2):
        across[i * columns : (i + 1) * columns] = wide
        down[:, i * group : (i + 1) * group] = tall
    cour[pl.ds(here, half)] = own_courant[...]
    cour[pl.ds(there, half)] = far_courant[...]

    def turn(h, carry):
        for source, start in ((own_reflect, here // stack), (far_reflect, there // stack)):
            for b in range(blocks // 2):
                tile = jnp.concatenate([source[h, stack * b + i] for i in range(stack)], 0)
                rt[h, start + b] = tile.astype(F32).T.astype(BF16)
        return carry

    lax.fori_loop(0, offsets, turn, 0)


def vertical(plane_of, z, depth, planes):
    total = EXACT_WEIGHTS[0] * plane_of(z)
    for k in range(1, REACH + 1):
        near = [plane_of(n) for n in (z - k, z + k) if 0 <= n < depth and n // planes != z // planes]
        if near:
            total = total + EXACT_WEIGHTS[k] * functools.reduce(jnp.add, near)
    return total


def sideways(terms, across, down):
    n = len(terms)
    group, columns = terms[0].shape
    x_part = jnp.dot(jnp.concatenate(terms, 1), across[0 : n * columns], preferred_element_type=F32)
    y_part = jnp.dot(down[:, 0 : n * group], jnp.concatenate(terms, 0), preferred_element_type=F32)
    return x_part + y_part


def source_of(lag_of, rt, cour, across, down, plain, shifted, turned, source):
    depth, rows, columns = cour.shape
    offsets, blocks = rt.shape[:2]
    group = down.shape[0]
    planes, tiles, stack = group // rows, group // 128, 128 // rows
    for g in range(depth // planes):
        high = jnp.concatenate([plain[g * planes + p].astype(BF16) for p in range(planes)], 0)
        both = sideways([high], across, down)
        for b in range(tiles):
            pieces = []
            for i in range(stack):
                p = b * stack + i
                z = g * planes + p
                upright = vertical(lambda n: plain[n], z, depth, planes)
                pieces.append(cour[z] * (both[p * rows : (p + 1) * rows] + upright))
            shifted[g * tiles + b, LAG : LAG + columns] = jnp.concatenate(pieces, 0).T
    chunk = 64
    for b in range(blocks):
        for r in range(0, columns, chunk):
            total = jnp.zeros((chunk, 128), F32)
            for h in range(offsets):
                image = rt[h, b, r : r + chunk].astype(F32)
                total = total + image * shifted[b, pl.ds(LAG + r - lag_of(h), chunk)]
            turned[b, r : r + chunk] = total
    for b in range(blocks):
        tile = turned[b].T
        for i in range(stack):
            source[stack * b + i] = tile[i * rows : (i + 1) * rows]


def clear_rims(shifted, columns):
    for b in range(shifted.shape[0]):
        shifted[b, 0:LAG] = jnp.zeros((LAG, 128), F32)
        shifted[b, LAG + columns : 2 * LAG + columns] = jnp.zeros((LAG, 128), F32)


def join_kernel(*refs):
    *parts, out = refs
    for i, part in enumerate(parts):
        out[i] = part[0]


def take_field(tests, core, plain):
    for test, at, own, far in tests:
        half = own.shape[1]

        @pl.when(test)
        def _(at=at, own=own, far=far, half=half):
            for z in range(half):
                plain[core * half + z] = own[at, z].astype(F32)
                plain[(1 - core) * half + z] = far[at, z].astype(F32)


def sums_kernel(groups, where_now, owners_ref, lags_ref, rt, cour, across, down, sums, plain, shifted, turned):
    first = where_now[1] * rt.shape[0]
    clear_rims(shifted, cour.shape[2])

    def any_of(tests):
        return functools.reduce(jnp.logical_or, [test for test, *_ in tests])

    def step(t, counts):
        taken, after = [], []
        for (choose, low, high), count in zip(groups, counts, strict=True):
            tests = choose(owners_ref[t] ^ where_now[0])
            due = (count >= low) & (count < high)
            taken += [(test & due, *bank) for test, *bank in tests]
            after.append(count + any_of(tests).astype(jnp.int32))

        @pl.when(any_of(taken))
        def _():
            take_field(taken, where_now[1], plain)
            source_of(lambda h: lags_ref[first + h], rt, cour, across, down, plain, shifted, turned, sums.at[t])

        return tuple(after)

    lax.fori_loop(0, ITERS, step, tuple(jnp.int32(0) for _ in groups))


def steps_kernel(
    groups, where_now, owners_ref, lags_ref, rt, cour, across, down, kept_ref, given_ref, sums,
    plain, shifted, turned, wave_a, wave_b,
):
    sums_kernel(
        groups, where_now, owners_ref, lags_ref, rt, cour, across, down, sums, plain, shifted, turned
    )
    depth, rows, _ = cour.shape
    half = depth // 2
    group = down.shape[0]
    planes = group // rows

    def grow(t, now, before):
        for g in range(depth // planes):
            high, low = split(jnp.concatenate([now[g * planes + p] for p in range(planes)], 0))
            both = sideways([high, low], across, down)
            for p in range(planes):
                z = g * planes + p
                laplace = both[p * rows : (p + 1) * rows] + vertical(lambda n: now[n], z, depth, planes)
                before[z] = (2.0 * now[z] - before[z]) + (cour[z] * laplace + sums[t, z])

    wave_a[...] = sums[0]
    wave_b[...] = jnp.zeros(wave_b.shape, F32)

    def pair(i, carry):
        grow(2 * i + 1, wave_a, wave_b)
        grow(2 * i + 2, wave_b, wave_a)
        return carry

    lax.fori_loop(0, (ITERS - 1) // 2, pair, 0)
    last = wave_a
    if ITERS % 2 == 0:
        grow(ITERS - 1, wave_a, wave_b)
        last = wave_b
    core = where_now[1]
    kept_ref[...] = last[pl.ds(core * half, half)]
    given_ref[...] = last[pl.ds((1 - core) * half, half)]


def swapped(x):
    return lax.ppermute(x, "dep", [(0, 1), (1, 0)])


def flip(x, bits):
    count = lax.axis_size("off")
    return lax.ppermute(x, "off", [(i, i ^ bits) for i in range(count)])


def core_pair(snapshots, reflect, courant, lags, owners):
    count = lax.axis_size("off")
    core = lax.axis_index("dep")
    mine = reflect.shape[0] // 2
    half, rows, columns = courant.shape
    depth = 2 * half
    blocks = depth * rows // 128
    group = 256
    wing = 4
    lines = count // wing

    z_parts = [flip(snapshots, wing * j) for j in range(1, lines)]
    o_x, o_y = flip(snapshots, 1), flip(snapshots, 2)
    o_d = flip(o_x, 2)
    sent = lax.dynamic_slice_in_dim(reflect, (1 - core) * mine, mine, 0)
    far_reflect = swapped(sent)
    own_reflect = lax.dynamic_slice_in_dim(reflect, core * mine, mine, 0)
    own_courant = courant * SCALE
    far_courant = swapped(own_courant)

    smem = pl.BlockSpec(memory_space=pltpu.SMEM)
    anyspace = pl.BlockSpec(memory_space=pl.ANY)
    vmem = pl.BlockSpec(memory_space=pltpu.VMEM)
    tables = [
        jax.ShapeDtypeStruct((mine, blocks, columns, 128), BF16),
        jax.ShapeDtypeStruct((depth, rows, columns), F32),
        jax.ShapeDtypeStruct((2 * columns, columns), BF16),
        jax.ShapeDtypeStruct((group, 2 * group), BF16),
    ]
    prepare = pl.pallas_call(
        prepare_kernel,
        out_shape=tables,
        in_specs=[vmem] * 4,
        out_specs=[vmem] * 4,
        compiler_params=pltpu.CompilerParams(vmem_limit_bytes=6 << 20),
        cost_estimate=pl.CostEstimate(flops=10**7, bytes_accessed=6 << 20, transcendentals=0),
    )
    prepared = prepare(own_reflect, far_reflect, own_courant, far_courant)
    z_shape = jax.ShapeDtypeStruct((lines - 1, half, rows, columns), BF16)
    small = pl.CostEstimate(flops=0, bytes_accessed=1 << 20, transcendentals=0)
    join = pl.pallas_call(
        join_kernel,
        out_shape=z_shape,
        in_specs=[vmem] * (lines - 1),
        out_specs=vmem,
        compiler_params=pltpu.CompilerParams(vmem_limit_bytes=2 << 20),
        cost_estimate=small,
    )
    z_all = join(*z_parts)
    z_x, z_y = flip(z_all, 1), flip(z_all, 2)
    d_parts = [flip(o_d, wing * j) for j in range(1, lines)]
    d_all = join(*d_parts)

    scratch = [
        pltpu.VMEM((depth, rows, columns), F32),
        pltpu.VMEM((blocks, columns + 2 * LAG, 128), F32),
        pltpu.VMEM((blocks, columns, 128), F32),
    ]
    waves = [pltpu.VMEM((depth, rows, columns), F32)] * 2
    params = pltpu.CompilerParams(vmem_limit_bytes=6 << 20)
    cost = pl.CostEstimate(flops=10**9, bytes_accessed=10 << 20, transcendentals=0)
    sums_shape = jax.ShapeDtypeStruct((ITERS, depth, rows, columns), F32)

    def near_banks(owns, fars):
        def choose(apart):
            low, line = apart % wing, apart // wing
            own_line = [((line == 0) & (low == i), 0, owns[i], fars[i]) for i in range(wing)]
            return own_line + [((line > 0) & (low == 0), line - 1, owns[wing], fars[wing])]

        return choose

    def side_banks(owns, fars):
        def choose(apart):
            low, line = apart % wing, apart // wing
            return [((line > 0) & (low == 1 + i), line - 1, owns[i], fars[i]) for i in range(2)]

        return choose

    def far_banks(owns, fars):
        def choose(apart):
            low, line = apart % wing, apart // wing
            return [((low == 3) & (line > 0), line - 1, owns[0], fars[0])]

        return choose

    def both_halves(own_parts):
        return own_parts, [swapped(v) for v in own_parts]

    def run(body, groups, extra, out_shape, more_scratch=()):
        arrays = [v for (owns, fars), *_ in groups for v in [*owns, *fars]]
        n = len(arrays)

        def kernel(owners_ref, lags_ref, *refs):
            where_now = lax.axis_index("off"), lax.axis_index("dep")
            given, chosen = list(refs[:n]), []
            for (owns, fars), banks, low, high in groups:
                own_refs = [given.pop(0) for _ in owns]
                far_refs = [given.pop(0) for _ in fars]
                chosen.append((banks(own_refs, far_refs), low, high))
            rest = refs[n : n + 4] + refs[n + 4 + len(extra) :]
            body(chosen, where_now, owners_ref, lags_ref, *rest)

        return pl.pallas_call(
            kernel,
            in_specs=[smem] * 2 + [vmem] * (n + 4 + len(extra)),
            out_shape=out_shape,
            out_specs=[vmem] * len(out_shape),
            scratch_shapes=scratch + list(more_scratch),
            input_output_aliases={2 + n + 4: len(out_shape) - 1} if extra else {},
            compiler_params=params,
            cost_estimate=cost,
        )(owners, lags, *arrays, *prepared, *extra)

    out_half = jax.ShapeDtypeStruct((half, rows, columns), F32)
    near = both_halves([snapshots, o_x, o_y, o_d, z_all])
    side = both_halves([z_x, z_y])
    far = both_halves([d_all])
    sums = run(sums_kernel, [(near, near_banks, 0, ITERS)], [], [sums_shape])
    sums = run(sums_kernel, [(side, side_banks, 0, ITERS)], sums, [sums_shape])
    groups = [(far, far_banks, 0, ITERS)]
    kept, given, _ = run(steps_kernel, groups, sums, [out_half, out_half, sums_shape], waves)

    total = kept + swapped(given)
    pieces = total.reshape(count, half * rows // count, columns)
    summed = lax.all_to_all(pieces, "off", 0, 0).sum(0)
    spread = jnp.broadcast_to(summed[None], pieces.shape)
    return lax.all_to_all(spread, "off", 0, 0).reshape(half, rows, columns)


def solution(mesh):
    offs, deps = mesh.shape["off"], mesh.shape["dep"]

    def per_device(snapshots, reflect, courant, lags, owners):
        fits = (
            deps == 2
            and snapshots.shape[0] == 1
            and offs >= 16
            and offs & (offs - 1) == 0
            and reflect.shape[0] % 2 == 0
            and courant.shape[2] % 128 == 0
            and (courant.shape[0] * courant.shape[1]) % (8 * offs) == 0
            and (courant.shape[0] * courant.shape[1]) % 128 == 0
            and courant.shape[1] % 16 == 0
            and 128 % courant.shape[1] == 0
        )
        body = core_pair if fits else halo_steps
        return body(snapshots, reflect, courant, lags, owners)

    in_specs = (
        P("off", "dep", None, None),
        P("off", "dep", None, None),
        P("dep", None, None),
        P("off"),
        P(),
    )
    return jax.shard_map(
        per_device, mesh=mesh, in_specs=in_specs, out_specs=P("dep", None, None), check_vma=False
    )
```

```python
import functools

import jax
import jax.numpy as jnp
from jax import lax
from jax.experimental import pallas as pl
from jax.experimental.pallas import tpu as pltpu
from jax.sharding import PartitionSpec as P


ITERS = 8
LAG = 32
REACH = 4

STENCIL_WEIGHTS = (-205.0 / 72.0, 8.0 / 5.0, -1.0 / 5.0, 8.0 / 315.0, -1.0 / 560.0)


BF16 = jnp.bfloat16
F32 = jnp.float32


def extended(cells, sides, width):
    for axis, dim in sides:
        count = lax.axis_size(axis)
        ends = count - 1
        head = lax.slice_in_dim(cells, 0, width, axis=dim)
        tail = lax.slice_in_dim(cells, cells.shape[dim] - width, cells.shape[dim], axis=dim)
        cells = jnp.concatenate(
            [
                lax.ppermute(tail, axis, [(i, (i + 1) % count) for i in range(ends)]),
                cells,
                lax.ppermute(head, axis, [((i + 1) % count, i) for i in range(ends)]),
            ],
            axis=dim,
        )
    return cells


def broadcast(x, axis, root):
    mine = lax.axis_index(axis) == root
    return lax.psum(jnp.where(mine, x, jnp.zeros_like(x)), axis)


def stencil(padded, depth_cells, row_cells, column_cells):
    def part(dz, dy, dx):
        return padded[
            4 + dz : 4 + dz + depth_cells, 4 + dy : 4 + dy + row_cells, 4 + dx : 4 + dx + column_cells
        ]

    summed = 3.0 * STENCIL_WEIGHTS[0] * part(0, 0, 0)
    for k in range(1, 5):
        neighbours = part(k, 0, 0) + part(-k, 0, 0)
        neighbours = neighbours + part(0, k, 0) + part(0, -k, 0)
        neighbours = neighbours + part(0, 0, k) + part(0, 0, -k)
        summed = summed + STENCIL_WEIGHTS[k] * neighbours
    return summed


def shifted_sum(reflect, acceleration, lags):
    width_cells = acceleration.shape[2]
    padded = jnp.pad(acceleration, ((0, 0), (0, 0), (LAG, LAG)))

    def add_offset(offset_index, summed):
        lag_now = lags[offset_index]
        window = lax.dynamic_slice_in_dim(padded, LAG - lag_now, width_cells, 2)
        return summed + reflect[offset_index].astype(F32) * window

    return lax.fori_loop(0, reflect.shape[0], add_offset, jnp.zeros(acceleration.shape, F32))


def halo_steps(snapshots, reflect, courant, lags, owners):
    own_layers = extended(snapshots[0], (("dep", 0),), 4)
    own_ready = courant * stencil(
        jnp.pad(own_layers, ((0, 0), (4, 4), (4, 4))).astype(F32), *courant.shape
    )
    scattered = jnp.zeros(courant.shape, F32)
    previous = jnp.zeros(courant.shape, F32)
    for step_now in range(ITERS):
        acceleration = broadcast(own_ready, "off", owners[step_now])
        source = shifted_sum(reflect, acceleration, lags)
        field = jnp.pad(extended(scattered, (("dep", 0),), 4), ((0, 0), (4, 4), (4, 4)))
        updated = 2.0 * scattered - previous + courant * stencil(field, *courant.shape) + source
        previous = scattered
        scattered = updated
    return lax.psum(scattered, "off")


def split(v):
    high = v.astype(BF16)
    return high, (v - high.astype(F32)).astype(BF16)


EXACT_WEIGHTS = tuple(w / 4096.0 for w in (-43050.0, 8064.0, -1008.0, 128.0, -9.0))
SCALE = 4096.0 / 5040.0


def band(rows, columns, block):
    i = lax.broadcasted_iota(jnp.int32, (rows, columns), 0)
    j = lax.broadcasted_iota(jnp.int32, (rows, columns), 1)
    blocks_apart, cells_apart = jnp.abs(i // block - j // block), jnp.abs(i % block - j % block)
    apart = jnp.where(blocks_apart == 0, cells_apart, jnp.where(cells_apart == 0, blocks_apart, 0))
    full = jnp.zeros((rows, columns), F32)
    for k in range(1, REACH + 1):
        full = jnp.where(apart == k, EXACT_WEIGHTS[k], full)
    return full.astype(BF16)


def prepare_kernel(own_reflect, far_reflect, own_courant, far_courant, rt, cour, across, down):
    core = lax.axis_index("dep")
    half, rows, columns = own_courant.shape
    offsets, blocks = rt.shape[:2]
    stack = 128 // rows
    here, there = core * half, (1 - core) * half
    wide = band(columns, columns, columns)
    group = down.shape[0]
    tall = band(group, group, rows)
    for i in range(2):
        across[i * columns : (i + 1) * columns] = wide
        down[:, i * group : (i + 1) * group] = tall
    cour[pl.ds(here, half)] = own_courant[...]
    cour[pl.ds(there, half)] = far_courant[...]

    def turn(h, carry):
        for source, start in ((own_reflect, here // stack), (far_reflect, there // stack)):
            for b in range(blocks // 2):
                tile = jnp.concatenate([source[h, stack * b + i] for i in range(stack)], 0)
                rt[h, start + b] = tile.astype(F32).T.astype(BF16)
        return carry

    lax.fori_loop(0, offsets, turn, 0)


def vertical(plane_of, z, depth, planes):
    total = EXACT_WEIGHTS[0] * plane_of(z)
    for k in range(1, REACH + 1):
        near = [plane_of(n) for n in (z - k, z + k) if 0 <= n < depth and n // planes != z // planes]
        if near:
            total = total + EXACT_WEIGHTS[k] * functools.reduce(jnp.add, near)
    return total


def sideways(terms, across, down):
    n = len(terms)
    group, columns = terms[0].shape
    x_part = jnp.dot(jnp.concatenate(terms, 1), across[0 : n * columns], preferred_element_type=F32)
    y_part = jnp.dot(down[:, 0 : n * group], jnp.concatenate(terms, 0), preferred_element_type=F32)
    return x_part + y_part


def source_of(lag_of, rt, cour, across, down, plain, shifted, turned, source):
    depth, rows, columns = cour.shape
    offsets, blocks = rt.shape[:2]
    group = down.shape[0]
    planes, tiles, stack = group // rows, group // 128, 128 // rows
    for g in range(depth // planes):
        high = jnp.concatenate([plain[g * planes + p].astype(BF16) for p in range(planes)], 0)
        both = sideways([high], across, down)
        for b in range(tiles):
            pieces = []
            for i in range(stack):
                p = b * stack + i
                z = g * planes + p
                upright = vertical(lambda n: plain[n], z, depth, planes)
                pieces.append(cour[z] * (both[p * rows : (p + 1) * rows] + upright))
            shifted[g * tiles + b, LAG : LAG + columns] = jnp.concatenate(pieces, 0).T
    chunk = 64
    for b in range(blocks):
        for r in range(0, columns, chunk):
            total = jnp.zeros((chunk, 128), F32)
            for h in range(offsets):
                image = rt[h, b, r : r + chunk].astype(F32)
                total = total + image * shifted[b, pl.ds(LAG + r - lag_of(h), chunk)]
            turned[b, r : r + chunk] = total
    for b in range(blocks):
        tile = turned[b].T
        for i in range(stack):
            source[stack * b + i] = tile[i * rows : (i + 1) * rows]


def clear_rims(shifted, columns):
    for b in range(shifted.shape[0]):
        shifted[b, 0:LAG] = jnp.zeros((LAG, 128), F32)
        shifted[b, LAG + columns : 2 * LAG + columns] = jnp.zeros((LAG, 128), F32)


def join_kernel(*refs):
    *parts, out = refs
    for i, part in enumerate(parts):
        out[i] = part[0]


def take_field(tests, core, plain):
    for test, at, own, far in tests:
        half = own.shape[1]

        @pl.when(test)
        def _(at=at, own=own, far=far, half=half):
            for z in range(half):
                plain[core * half + z] = own[at, z].astype(F32)
                plain[(1 - core) * half + z] = far[at, z].astype(F32)


def first_with_owner(owners_ref, t):
    first = t
    for s in reversed(range(ITERS)):
        first = jnp.where((s < t) & (owners_ref[s] == owners_ref[t]), s, first)
    return first


def sums_kernel(groups, where_now, owners_ref, lags_ref, rt, cour, across, down, sums, plain, shifted, turned):
    first = where_now[1] * rt.shape[0]
    clear_rims(shifted, cour.shape[2])

    def any_of(tests):
        return functools.reduce(jnp.logical_or, [test for test, *_ in tests])

    def step(t, counts):
        taken, after = [], []
        fresh = first_with_owner(owners_ref, t) == t
        for (choose, low, high), count in zip(groups, counts, strict=True):
            tests = choose(owners_ref[t] ^ where_now[0])
            due = fresh & (count >= low) & (count < high)
            taken += [(test & due, *bank) for test, *bank in tests]
            after.append(count + any_of(tests).astype(jnp.int32))

        @pl.when(any_of(taken))
        def _():
            take_field(taken, where_now[1], plain)
            source_of(lambda h: lags_ref[first + h], rt, cour, across, down, plain, shifted, turned, sums.at[t])

        return tuple(after)

    lax.fori_loop(0, ITERS, step, tuple(jnp.int32(0) for _ in groups))


def steps_kernel(
    groups, where_now, owners_ref, lags_ref, rt, cour, across, down, kept_ref, given_ref, sums,
    plain, shifted, turned, wave_a, wave_b,
):
    sums_kernel(
        groups, where_now, owners_ref, lags_ref, rt, cour, across, down, sums, plain, shifted, turned
    )
    depth, rows, _ = cour.shape
    half = depth // 2
    group = down.shape[0]
    planes = group // rows

    def grow(t, now, before):
        served = first_with_owner(owners_ref, t)
        for g in range(depth // planes):
            high, low = split(jnp.concatenate([now[g * planes + p] for p in range(planes)], 0))
            both = sideways([high, low], across, down)
            for p in range(planes):
                z = g * planes + p
                laplace = both[p * rows : (p + 1) * rows] + vertical(lambda n: now[n], z, depth, planes)
                before[z] = (2.0 * now[z] - before[z]) + (cour[z] * laplace + sums[served, z])

    wave_a[...] = sums[0]
    wave_b[...] = jnp.zeros(wave_b.shape, F32)

    def pair(i, carry):
        grow(2 * i + 1, wave_a, wave_b)
        grow(2 * i + 2, wave_b, wave_a)
        return carry

    lax.fori_loop(0, (ITERS - 1) // 2, pair, 0)
    last = wave_a
    if ITERS % 2 == 0:
        grow(ITERS - 1, wave_a, wave_b)
        last = wave_b
    core = where_now[1]
    kept_ref[...] = last[pl.ds(core * half, half)]
    given_ref[...] = last[pl.ds((1 - core) * half, half)]


def swapped(x):
    return lax.ppermute(x, "dep", [(0, 1), (1, 0)])


def flip(x, bits):
    count = lax.axis_size("off")
    return lax.ppermute(x, "off", [(i, i ^ bits) for i in range(count)])


def core_pair(snapshots, reflect, courant, lags, owners):
    count = lax.axis_size("off")
    core = lax.axis_index("dep")
    mine = reflect.shape[0] // 2
    half, rows, columns = courant.shape
    depth = 2 * half
    blocks = depth * rows // 128
    group = 256
    wing = 4
    lines = count // wing

    z_parts = [flip(snapshots, wing * j) for j in range(1, lines)]
    o_x, o_y = flip(snapshots, 1), flip(snapshots, 2)
    o_d = flip(o_x, 2)
    sent = lax.dynamic_slice_in_dim(reflect, (1 - core) * mine, mine, 0)
    far_reflect = swapped(sent)
    own_reflect = lax.dynamic_slice_in_dim(reflect, core * mine, mine, 0)
    own_courant = courant * SCALE
    far_courant = swapped(own_courant)

    smem = pl.BlockSpec(memory_space=pltpu.SMEM)
    anyspace = pl.BlockSpec(memory_space=pl.ANY)
    vmem = pl.BlockSpec(memory_space=pltpu.VMEM)
    tables = [
        jax.ShapeDtypeStruct((mine, blocks, columns, 128), BF16),
        jax.ShapeDtypeStruct((depth, rows, columns), F32),
        jax.ShapeDtypeStruct((2 * columns, columns), BF16),
        jax.ShapeDtypeStruct((group, 2 * group), BF16),
    ]
    prepare = pl.pallas_call(
        prepare_kernel,
        out_shape=tables,
        in_specs=[vmem] * 4,
        out_specs=[vmem] * 4,
        compiler_params=pltpu.CompilerParams(vmem_limit_bytes=6 << 20),
        cost_estimate=pl.CostEstimate(flops=10**7, bytes_accessed=6 << 20, transcendentals=0),
    )
    prepared = prepare(own_reflect, far_reflect, own_courant, far_courant)
    z_shape = jax.ShapeDtypeStruct((lines - 1, half, rows, columns), BF16)
    small = pl.CostEstimate(flops=0, bytes_accessed=1 << 20, transcendentals=0)
    join = pl.pallas_call(
        join_kernel,
        out_shape=z_shape,
        in_specs=[vmem] * (lines - 1),
        out_specs=vmem,
        compiler_params=pltpu.CompilerParams(vmem_limit_bytes=2 << 20),
        cost_estimate=small,
    )
    z_all = join(*z_parts)
    z_x, z_y = flip(z_all, 1), flip(z_all, 2)
    d_parts = [flip(o_d, wing * j) for j in range(1, lines)]
    d_all = join(*d_parts)

    scratch = [
        pltpu.VMEM((depth, rows, columns), F32),
        pltpu.VMEM((blocks, columns + 2 * LAG, 128), F32),
        pltpu.VMEM((blocks, columns, 128), F32),
    ]
    waves = [pltpu.VMEM((depth, rows, columns), F32)] * 2
    params = pltpu.CompilerParams(vmem_limit_bytes=6 << 20)
    cost = pl.CostEstimate(flops=10**9, bytes_accessed=10 << 20, transcendentals=0)
    sums_shape = jax.ShapeDtypeStruct((ITERS, depth, rows, columns), F32)

    def near_banks(owns, fars):
        def choose(apart):
            low, line = apart % wing, apart // wing
            own_line = [((line == 0) & (low == i), 0, owns[i], fars[i]) for i in range(wing)]
            return own_line + [((line > 0) & (low == 0), line - 1, owns[wing], fars[wing])]

        return choose

    def side_banks(owns, fars):
        def choose(apart):
            low, line = apart % wing, apart // wing
            return [((line > 0) & (low == 1 + i), line - 1, owns[i], fars[i]) for i in range(2)]

        return choose

    def far_banks(owns, fars):
        def choose(apart):
            low, line = apart % wing, apart // wing
            return [((low == 3) & (line > 0), line - 1, owns[0], fars[0])]

        return choose

    def both_halves(own_parts):
        return own_parts, [swapped(v) for v in own_parts]

    def run(body, groups, extra, out_shape, more_scratch=()):
        arrays = [v for (owns, fars), *_ in groups for v in [*owns, *fars]]
        n = len(arrays)

        def kernel(owners_ref, lags_ref, *refs):
            where_now = lax.axis_index("off"), lax.axis_index("dep")
            given, chosen = list(refs[:n]), []
            for (owns, fars), banks, low, high in groups:
                own_refs = [given.pop(0) for _ in owns]
                far_refs = [given.pop(0) for _ in fars]
                chosen.append((banks(own_refs, far_refs), low, high))
            rest = refs[n : n + 4] + refs[n + 4 + len(extra) :]
            body(chosen, where_now, owners_ref, lags_ref, *rest)

        return pl.pallas_call(
            kernel,
            in_specs=[smem] * 2 + [vmem] * (n + 4 + len(extra)),
            out_shape=out_shape,
            out_specs=[vmem] * len(out_shape),
            scratch_shapes=scratch + list(more_scratch),
            input_output_aliases={2 + n + 4: len(out_shape) - 1} if extra else {},
            compiler_params=params,
            cost_estimate=cost,
        )(owners, lags, *arrays, *prepared, *extra)

    out_half = jax.ShapeDtypeStruct((half, rows, columns), F32)
    near = both_halves([snapshots, o_x, o_y, o_d, z_all])
    side = both_halves([z_x, z_y])
    far = both_halves([d_all])
    sums = run(sums_kernel, [(near, near_banks, 0, ITERS)], [], [sums_shape])
    sums = run(sums_kernel, [(side, side_banks, 0, ITERS)], sums, [sums_shape])
    groups = [(far, far_banks, 0, ITERS)]
    kept, given, _ = run(steps_kernel, groups, sums, [out_half, out_half, sums_shape], waves)

    total = kept + swapped(given)
    pieces = total.reshape(count, half * rows // count, columns)
    summed = lax.all_to_all(pieces, "off", 0, 0).sum(0)
    spread = jnp.broadcast_to(summed[None], pieces.shape)
    return lax.all_to_all(spread, "off", 0, 0).reshape(half, rows, columns)


def solution(mesh):
    offs, deps = mesh.shape["off"], mesh.shape["dep"]

    def per_device(snapshots, reflect, courant, lags, owners):
        fits = (
            deps == 2
            and snapshots.shape[0] == 1
            and offs >= 16
            and offs & (offs - 1) == 0
            and reflect.shape[0] % 2 == 0
            and courant.shape[2] % 128 == 0
            and (courant.shape[0] * courant.shape[1]) % (8 * offs) == 0
            and (courant.shape[0] * courant.shape[1]) % 128 == 0
            and courant.shape[1] % 16 == 0
            and 128 % courant.shape[1] == 0
        )
        body = core_pair if fits else halo_steps
        return body(snapshots, reflect, courant, lags, owners)

    in_specs = (
        P("off", "dep", None, None),
        P("off", "dep", None, None),
        P("dep", None, None),
        P("off"),
        P(),
    )
    return jax.shard_map(
        per_device, mesh=mesh, in_specs=in_specs, out_specs=P("dep", None, None), check_vma=False
    )
```

```python
import functools

import jax
import jax.numpy as jnp
from jax import lax
from jax.experimental import pallas as pl
from jax.experimental.pallas import tpu as pltpu
from jax.sharding import PartitionSpec as P


ITERS = 8
LAG = 32
REACH = 4

STENCIL_WEIGHTS = (-205.0 / 72.0, 8.0 / 5.0, -1.0 / 5.0, 8.0 / 315.0, -1.0 / 560.0)


BF16 = jnp.bfloat16
F32 = jnp.float32


def extended(cells, sides, width):
    for axis, dim in sides:
        count = lax.axis_size(axis)
        ends = count - 1
        head = lax.slice_in_dim(cells, 0, width, axis=dim)
        tail = lax.slice_in_dim(cells, cells.shape[dim] - width, cells.shape[dim], axis=dim)
        cells = jnp.concatenate(
            [
                lax.ppermute(tail, axis, [(i, (i + 1) % count) for i in range(ends)]),
                cells,
                lax.ppermute(head, axis, [((i + 1) % count, i) for i in range(ends)]),
            ],
            axis=dim,
        )
    return cells


def broadcast(x, axis, root):
    mine = lax.axis_index(axis) == root
    return lax.psum(jnp.where(mine, x, jnp.zeros_like(x)), axis)


def stencil(padded, depth_cells, row_cells, column_cells):
    def part(dz, dy, dx):
        return padded[
            4 + dz : 4 + dz + depth_cells, 4 + dy : 4 + dy + row_cells, 4 + dx : 4 + dx + column_cells
        ]

    summed = 3.0 * STENCIL_WEIGHTS[0] * part(0, 0, 0)
    for k in range(1, 5):
        neighbours = part(k, 0, 0) + part(-k, 0, 0)
        neighbours = neighbours + part(0, k, 0) + part(0, -k, 0)
        neighbours = neighbours + part(0, 0, k) + part(0, 0, -k)
        summed = summed + STENCIL_WEIGHTS[k] * neighbours
    return summed


def shifted_sum(reflect, acceleration, lags):
    width_cells = acceleration.shape[2]
    padded = jnp.pad(acceleration, ((0, 0), (0, 0), (LAG, LAG)))

    def add_offset(offset_index, summed):
        lag_now = lags[offset_index]
        window = lax.dynamic_slice_in_dim(padded, LAG - lag_now, width_cells, 2)
        return summed + reflect[offset_index].astype(F32) * window

    return lax.fori_loop(0, reflect.shape[0], add_offset, jnp.zeros(acceleration.shape, F32))


def halo_steps(snapshots, reflect, courant, lags, owners):
    own_layers = extended(snapshots[0], (("dep", 0),), 4)
    own_ready = courant * stencil(
        jnp.pad(own_layers, ((0, 0), (4, 4), (4, 4))).astype(F32), *courant.shape
    )
    scattered = jnp.zeros(courant.shape, F32)
    previous = jnp.zeros(courant.shape, F32)
    for step_now in range(ITERS):
        acceleration = broadcast(own_ready, "off", owners[step_now])
        source = shifted_sum(reflect, acceleration, lags)
        field = jnp.pad(extended(scattered, (("dep", 0),), 4), ((0, 0), (4, 4), (4, 4)))
        updated = 2.0 * scattered - previous + courant * stencil(field, *courant.shape) + source
        previous = scattered
        scattered = updated
    return lax.psum(scattered, "off")


def split(v):
    high = v.astype(BF16)
    return high, (v - high.astype(F32)).astype(BF16)


EXACT_WEIGHTS = tuple(w / 4096.0 for w in (-43050.0, 8064.0, -1008.0, 128.0, -9.0))
SCALE = 4096.0 / 5040.0


def band(rows, columns, block):
    i = lax.broadcasted_iota(jnp.int32, (rows, columns), 0)
    j = lax.broadcasted_iota(jnp.int32, (rows, columns), 1)
    blocks_apart, cells_apart = jnp.abs(i // block - j // block), jnp.abs(i % block - j % block)
    apart = jnp.where(blocks_apart == 0, cells_apart, jnp.where(cells_apart == 0, blocks_apart, 0))
    full = jnp.zeros((rows, columns), F32)
    for k in range(1, REACH + 1):
        full = jnp.where(apart == k, EXACT_WEIGHTS[k], full)
    return full.astype(BF16)


def prepare_kernel(own_reflect, far_reflect, own_courant, far_courant, rt, cour, across, down):
    core = lax.axis_index("dep")
    half, rows, columns = own_courant.shape
    offsets, blocks = rt.shape[:2]
    stack = 128 // rows
    here, there = core * half, (1 - core) * half
    wide = band(columns, columns, columns)
    group = down.shape[0]
    tall = band(group, group, rows)
    for i in range(2):
        across[i * columns : (i + 1) * columns] = wide
        down[:, i * group : (i + 1) * group] = tall
    cour[pl.ds(here, half)] = own_courant[...]
    cour[pl.ds(there, half)] = far_courant[...]

    def turn(h, carry):
        for source, start in ((own_reflect, here // stack), (far_reflect, there // stack)):
            for b in range(blocks // 2):
                tile = jnp.concatenate([source[h, stack * b + i] for i in range(stack)], 0)
                rt[h, start + b] = tile.astype(F32).T.astype(BF16)
        return carry

    lax.fori_loop(0, offsets, turn, 0)


def vertical(plane_of, z, depth, planes):
    total = EXACT_WEIGHTS[0] * plane_of(z)
    for k in range(1, REACH + 1):
        near = [plane_of(n) for n in (z - k, z + k) if 0 <= n < depth and n // planes != z // planes]
        if near:
            total = total + EXACT_WEIGHTS[k] * functools.reduce(jnp.add, near)
    return total


def sideways(terms, across, down):
    n = len(terms)
    group, columns = terms[0].shape
    x_part = jnp.dot(jnp.concatenate(terms, 1), across[0 : n * columns], preferred_element_type=F32)
    y_part = jnp.dot(down[:, 0 : n * group], jnp.concatenate(terms, 0), preferred_element_type=F32)
    return x_part + y_part


def source_of(lag_of, rt, cour, across, down, plain, shifted, turned, source):
    depth, rows, columns = cour.shape
    offsets, blocks = rt.shape[:2]
    group = down.shape[0]
    planes, tiles, stack = group // rows, group // 128, 128 // rows
    for g in range(depth // planes):
        high = jnp.concatenate([plain[g * planes + p].astype(BF16) for p in range(planes)], 0)
        both = sideways([high], across, down)
        for b in range(tiles):
            pieces = []
            for i in range(stack):
                p = b * stack + i
                z = g * planes + p
                upright = vertical(lambda n: plain[n], z, depth, planes)
                pieces.append(cour[z] * (both[p * rows : (p + 1) * rows] + upright))
            shifted[g * tiles + b, LAG : LAG + columns] = jnp.concatenate(pieces, 0).T
    chunk = 64
    for b in range(blocks):
        for r in range(0, columns, chunk):
            total = jnp.zeros((chunk, 128), F32)
            for h in range(offsets):
                image = rt[h, b, r : r + chunk].astype(F32)
                total = total + image * shifted[b, pl.ds(LAG + r - lag_of(h), chunk)]
            turned[b, r : r + chunk] = total
    for b in range(blocks):
        tile = turned[b].T
        for i in range(stack):
            source[stack * b + i] = tile[i * rows : (i + 1) * rows]


def clear_rims(shifted, columns):
    for b in range(shifted.shape[0]):
        shifted[b, 0:LAG] = jnp.zeros((LAG, 128), F32)
        shifted[b, LAG + columns : 2 * LAG + columns] = jnp.zeros((LAG, 128), F32)


def join_kernel(*refs):
    *parts, out = refs
    for i, part in enumerate(parts):
        out[i] = part[0]


def take_field(tests, core, plain):
    for test, at, own, far in tests:
        half = own.shape[1]

        @pl.when(test)
        def _(at=at, own=own, far=far, half=half):
            for z in range(half):
                plain[core * half + z] = own[at, z].astype(F32)
                plain[(1 - core) * half + z] = far[at, z].astype(F32)


def first_with_owner(owners_ref, t):
    first = t
    for s in reversed(range(ITERS)):
        first = jnp.where((s < t) & (owners_ref[s] == owners_ref[t]), s, first)
    return first


def sums_kernel(groups, where_now, owners_ref, lags_ref, rt, cour, across, down, sums, plain, shifted, turned):
    first = where_now[1] * rt.shape[0]
    clear_rims(shifted, cour.shape[2])

    def any_of(tests):
        return functools.reduce(jnp.logical_or, [test for test, *_ in tests])

    def step(t, counts):
        taken, after = [], []
        fresh = first_with_owner(owners_ref, t) == t
        for (choose, low, high), count in zip(groups, counts, strict=True):
            tests = choose(owners_ref[t] ^ where_now[0])
            due = fresh & (count >= low) & (count < high)
            taken += [(test & due, *bank) for test, *bank in tests]
            after.append(count + any_of(tests).astype(jnp.int32))

        @pl.when(any_of(taken))
        def _():
            take_field(taken, where_now[1], plain)
            source_of(lambda h: lags_ref[first + h], rt, cour, across, down, plain, shifted, turned, sums.at[t])

        return tuple(after)

    lax.fori_loop(0, ITERS, step, tuple(jnp.int32(0) for _ in groups))


def steps_kernel(
    groups, where_now, owners_ref, lags_ref, rt, cour, across, down, kept_ref, given_ref, sums,
    plain, shifted, turned, wave_a, wave_b,
):
    sums_kernel(
        groups, where_now, owners_ref, lags_ref, rt, cour, across, down, sums, plain, shifted, turned
    )
    depth, rows, _ = cour.shape
    half = depth // 2
    group = down.shape[0]
    planes = group // rows

    def grow(t, now, before):
        served = first_with_owner(owners_ref, t)
        for g in range(depth // planes):
            high, low = split(jnp.concatenate([now[g * planes + p] for p in range(planes)], 0))
            both = sideways([high, low], across, down)
            for p in range(planes):
                z = g * planes + p
                laplace = both[p * rows : (p + 1) * rows] + vertical(lambda n: now[n], z, depth, planes)
                before[z] = (2.0 * now[z] - before[z]) + (cour[z] * laplace + sums[served, z])

    wave_a[...] = sums[0]
    wave_b[...] = jnp.zeros(wave_b.shape, F32)

    def pair(i, carry):
        grow(2 * i + 1, wave_a, wave_b)
        grow(2 * i + 2, wave_b, wave_a)
        return carry

    lax.fori_loop(0, (ITERS - 1) // 2, pair, 0)
    last = wave_a
    if ITERS % 2 == 0:
        grow(ITERS - 1, wave_a, wave_b)
        last = wave_b
    core = where_now[1]
    kept_ref[...] = last[pl.ds(core * half, half)]
    given_ref[...] = last[pl.ds((1 - core) * half, half)]


def swapped(x):
    return lax.ppermute(x, "dep", [(0, 1), (1, 0)])


def flip(x, bits):
    count = lax.axis_size("off")
    return lax.ppermute(x, "off", [(i, i ^ bits) for i in range(count)])


def core_pair(snapshots, reflect, courant, lags, owners):
    count = lax.axis_size("off")
    core = lax.axis_index("dep")
    mine = reflect.shape[0] // 2
    half, rows, columns = courant.shape
    depth = 2 * half
    blocks = depth * rows // 128
    group = 256
    wing = 4
    lines = count // wing

    z_parts = [flip(snapshots, wing * j) for j in range(1, lines)]
    o_x, o_y = flip(snapshots, 1), flip(snapshots, 2)
    o_d = flip(o_x, 2)
    sent = lax.dynamic_slice_in_dim(reflect, (1 - core) * mine, mine, 0)
    far_reflect = swapped(sent)
    own_reflect = lax.dynamic_slice_in_dim(reflect, core * mine, mine, 0)
    own_courant = courant * SCALE
    far_courant = swapped(own_courant)

    smem = pl.BlockSpec(memory_space=pltpu.SMEM)
    anyspace = pl.BlockSpec(memory_space=pl.ANY)
    vmem = pl.BlockSpec(memory_space=pltpu.VMEM)
    tables = [
        jax.ShapeDtypeStruct((mine, blocks, columns, 128), BF16),
        jax.ShapeDtypeStruct((depth, rows, columns), F32),
        jax.ShapeDtypeStruct((2 * columns, columns), BF16),
        jax.ShapeDtypeStruct((group, 2 * group), BF16),
    ]
    prepare = pl.pallas_call(
        prepare_kernel,
        out_shape=tables,
        in_specs=[vmem] * 4,
        out_specs=[vmem] * 4,
        compiler_params=pltpu.CompilerParams(vmem_limit_bytes=6 << 20),
        cost_estimate=pl.CostEstimate(flops=10**7, bytes_accessed=6 << 20, transcendentals=0),
    )
    prepared = prepare(own_reflect, far_reflect, own_courant, far_courant)
    z_shape = jax.ShapeDtypeStruct((lines - 1, half, rows, columns), BF16)
    small = pl.CostEstimate(flops=0, bytes_accessed=1 << 20, transcendentals=0)
    join = pl.pallas_call(
        join_kernel,
        out_shape=z_shape,
        in_specs=[vmem] * (lines - 1),
        out_specs=vmem,
        compiler_params=pltpu.CompilerParams(vmem_limit_bytes=2 << 20),
        cost_estimate=small,
    )
    z_all = join(*z_parts)
    z_x, z_y = flip(z_all, 1), flip(z_all, 2)
    d_parts = [flip(o_d, wing * j) for j in range(1, lines)]

    scratch = [
        pltpu.VMEM((depth, rows, columns), F32),
        pltpu.VMEM((blocks, columns + 2 * LAG, 128), F32),
        pltpu.VMEM((blocks, columns, 128), F32),
    ]
    waves = [pltpu.VMEM((depth, rows, columns), F32)] * 2
    params = pltpu.CompilerParams(vmem_limit_bytes=6 << 20)
    cost = pl.CostEstimate(flops=10**9, bytes_accessed=10 << 20, transcendentals=0)
    sums_shape = jax.ShapeDtypeStruct((ITERS, depth, rows, columns), F32)

    def near_banks(owns, fars):
        def choose(apart):
            low, line = apart % wing, apart // wing
            own_line = [((line == 0) & (low == i), 0, owns[i], fars[i]) for i in range(wing)]
            return own_line + [((line > 0) & (low == 0), line - 1, owns[wing], fars[wing])]

        return choose

    def side_banks(owns, fars):
        def choose(apart):
            low, line = apart % wing, apart // wing
            return [((line > 0) & (low == 1 + i), line - 1, owns[i], fars[i]) for i in range(2)]

        return choose

    def far_banks(owns, fars):
        def choose(apart):
            low, line = apart % wing, apart // wing
            return [((low == 3) & (line == 1 + i), 0, owns[i], fars[i]) for i in range(lines - 1)]

        return choose

    def both_halves(own_parts):
        return own_parts, [swapped(v) for v in own_parts]

    def run(body, groups, extra, out_shape, more_scratch=()):
        arrays = [v for (owns, fars), *_ in groups for v in [*owns, *fars]]
        n = len(arrays)

        def kernel(owners_ref, lags_ref, *refs):
            where_now = lax.axis_index("off"), lax.axis_index("dep")
            given, chosen = list(refs[:n]), []
            for (owns, fars), banks, low, high in groups:
                own_refs = [given.pop(0) for _ in owns]
                far_refs = [given.pop(0) for _ in fars]
                chosen.append((banks(own_refs, far_refs), low, high))
            rest = refs[n : n + 4] + refs[n + 4 + len(extra) :]
            body(chosen, where_now, owners_ref, lags_ref, *rest)

        return pl.pallas_call(
            kernel,
            in_specs=[smem] * 2 + [vmem] * (n + 4 + len(extra)),
            out_shape=out_shape,
            out_specs=[vmem] * len(out_shape),
            scratch_shapes=scratch + list(more_scratch),
            input_output_aliases={2 + n + 4: len(out_shape) - 1} if extra else {},
            compiler_params=params,
            cost_estimate=cost,
        )(owners, lags, *arrays, *prepared, *extra)

    out_half = jax.ShapeDtypeStruct((half, rows, columns), F32)
    near = both_halves([snapshots, o_x, o_y, o_d, z_all])
    side = both_halves([z_x, z_y])
    far = both_halves(d_parts)
    sums = run(sums_kernel, [(near, near_banks, 0, ITERS)], [], [sums_shape])
    sums = run(sums_kernel, [(side, side_banks, 0, ITERS)], sums, [sums_shape])
    groups = [(far, far_banks, 0, ITERS)]
    kept, given, _ = run(steps_kernel, groups, sums, [out_half, out_half, sums_shape], waves)

    total = kept + swapped(given)
    pieces = total.reshape(count, half * rows // count, columns)
    summed = lax.all_to_all(pieces, "off", 0, 0).sum(0)
    spread = jnp.broadcast_to(summed[None], pieces.shape)
    return lax.all_to_all(spread, "off", 0, 0).reshape(half, rows, columns)


def solution(mesh):
    offs, deps = mesh.shape["off"], mesh.shape["dep"]

    def per_device(snapshots, reflect, courant, lags, owners):
        fits = (
            deps == 2
            and snapshots.shape[0] == 1
            and offs >= 16
            and offs & (offs - 1) == 0
            and reflect.shape[0] % 2 == 0
            and courant.shape[2] % 128 == 0
            and (courant.shape[0] * courant.shape[1]) % (8 * offs) == 0
            and (courant.shape[0] * courant.shape[1]) % 128 == 0
            and courant.shape[1] % 16 == 0
            and 128 % courant.shape[1] == 0
        )
        body = core_pair if fits else halo_steps
        return body(snapshots, reflect, courant, lags, owners)

    in_specs = (
        P("off", "dep", None, None),
        P("off", "dep", None, None),
        P("dep", None, None),
        P("off"),
        P(),
    )
    return jax.shard_map(
        per_device, mesh=mesh, in_specs=in_specs, out_specs=P("dep", None, None), check_vma=False
    )
```
